256 devices in a mesh: seq: 32 (over z_hi, y, core), tp: 8 (over z_lo, x).
Axes of the slice: x: 4, y: 4, z: 8 (z_hi: 4, z_lo: 2; z = z_hi * 2 + z_lo), core: 2. Of those that a mesh axis runs over, the one named last changes fastest.
Arguments:
- hidden_in: bfloat16 [16384, 4608], P('seq', 'tp'), may hold values from -6 to 6
- pre_gain: float32 [4608], replicated, may hold values from 0.1 to 1.9
- post_gain: float32 [4608], replicated, may hold values from 0.1 to 1.9
- w_query: bfloat16 [4608, 2048], P(None, 'tp'), may hold values from -0.4375 to 0.4375
- key_weight: bfloat16 [4608, 1024], P(None, 'tp'), may hold values from -0.21875 to 0.21875
- value_weight: bfloat16 [4608, 1024], P(None, 'tp'), may hold values from -0.21875 to 0.21875
- w_out: bfloat16 [2048, 4608], P(None, 'tp'), may hold values from -0.125 to 0.125
- prefix_key_value_cache: bfloat16 [65536, 2, 1024], P('seq', None, 'tp'), may hold values from -15 to 15
- suffix_len: int32 [48], replicated, may hold values from 1 to 2048, 16384 in all
- request_order: int32 [48], replicated, may hold values from 0 to 47, each once
- request_prefix: int32 [48], replicated, may hold values from 0 to 3
- prefix_owner: int32 [4], replicated, may hold values from 0 to 31, as said below
Outputs:
- hidden_out: bfloat16 [16384, 4608], P('seq', 'tp')
The draws below stay inside these ranges and needn't reach their ends.
Inputs may be any that keep to these rules, and one draw needn't show every extreme that they name: `suffix_len`: the suffix lengths sum to 16384, and the longest is exactly 2048. `request_order`: every request appears exactly once. `prefix_owner`: the 4 owners are distinct, and the first and the last index of seq are among them.
All inputs are finite; a program needn't handle non-finite values.
Results may differ from the reference program's by a relative error of at most 0.011.
Values may be sent and summed in bfloat16 or wider, within the bound.
A program may use at most 128 MiB of HBM per device.

```python
import math
import jax
import jax.numpy as jnp
import numpy as np
from jax import lax

MODEL_WIDTH = 4608
QUERY_HEADS = 16
KEY_VALUE_HEADS = 8
HEAD_SIZE = 128
QSCALE = 144
PREFIX_LENGTH = 2048
NPRE = 4
REQS = 48
TOK_DEV = 512
SUFFIX_TOKENS = 16384
LONGEST_SUFFIX = 2048
N_SEQ = 32


def draw_prefix_owner(key, part):
    inner_key = jax.random.fold_in(key, 11)
    order_key = jax.random.fold_in(key, 23)
    inner = (jax.random.permutation(inner_key, N_SEQ - 2)[:NPRE - 2] + 1).astype(jnp.int32)
    ends = jnp.array([0, N_SEQ - 1], dtype=jnp.int32)
    owners = jnp.concatenate([ends, inner], axis=0).astype(jnp.int32)
    shuffle = jax.random.permutation(order_key, NPRE)
    return owners[shuffle].astype(jnp.int32)


def place_ends(values, rng, least, top_value):
    shape = values.shape
    spot = [jax.random.randint(jax.random.fold_in(rng, axis), (), 0, shape[axis]) for axis in range(len(shape))]
    values = values.at[tuple(spot)].set(least)
    longest = shape.index(max(shape))
    spot[longest] = (spot[longest] + 1) % shape[longest]
    return values.at[tuple(spot)].set(top_value)


def block_scale(stream_key, shape, split, smallest, top_value):
    loudness = 1.0
    for dim, shards_of in split:
        heights = jax.random.uniform(jax.random.fold_in(jax.random.fold_in(stream_key, 6), dim), (shards_of,), jnp.float32, smallest / len(split), top_value / len(split))
        loudness = loudness * jnp.repeat(jnp.exp(heights), shape[dim] // shards_of).reshape((-1,) + (1,) * (len(shape) - 1 - dim))
    return loudness


def split_up(amount, total, reach, lean):
    loads = [(1 << 20) // math.isqrt(grade ** lean) + 1 for grade in range(2, amount + 1)]
    surplus, holding = total - reach - (amount - 1), [1] * (amount - 1)
    while surplus > 0:
        candidates = [i for i in range(amount - 1) if holding[i] < reach]
        pool, left = sum([loads[i] for i in candidates]), surplus
        for i in candidates:
            extra = min(reach - holding[i], max(1, left * loads[i] // pool), surplus)
            holding[i] = holding[i] + extra
            surplus = surplus - extra
    return np.array([reach] + holding)


def ragged(key, count, total, reach, slope):
    if count == 2:
        one = jax.random.randint(key, (), max(1, total - reach), min(reach, total - 1) + 1)
        return jnp.stack([one, total - one])
    tallies = jnp.asarray(split_up(count, total, reach, slope), jnp.int32)
    twos = (count - 1) // 2
    source_of, taker = tallies[1:1 + 2 * twos:2], tallies[2:2 + 2 * twos:2]
    margin = jnp.minimum(source_of - 1, reach - taker)
    shifted = jax.random.randint(jax.random.fold_in(key, 1), (twos,), 0, 1 << 20) % (margin + 1)
    tallies = tallies.at[1:1 + 2 * twos:2].set(source_of - shifted).at[2:2 + 2 * twos:2].set(taker + shifted)
    return tallies[jax.random.permutation(jax.random.fold_in(key, 2), count)]


def noise(stream_key, dims, width, bound, pieces=(), kind=jnp.bfloat16):
    entries = width * jax.random.normal(stream_key, dims, jnp.float32)
    if pieces:
        entries = entries * block_scale(stream_key, dims, pieces, -0.22, 0.18)
    return jnp.clip(entries, -bound, bound).astype(kind)


def setup_inputs(seed: int = 0) -> dict:
    keys = jax.random.split(jax.random.key(seed), 13)
    hidden_in = noise(keys[0], (SUFFIX_TOKENS, MODEL_WIDTH), 1.0, 6.0, ((0, 32), (1, 8)))
    pre_gain = jnp.clip(1.0 + 0.18 * jax.random.normal(keys[1], (MODEL_WIDTH,), jnp.float32), 0.1, 1.9)
    post_gain = jnp.clip(1.0 + 0.18 * jax.random.normal(keys[2], (MODEL_WIDTH,), jnp.float32), 0.1, 1.9)
    w_query = noise(keys[3], (MODEL_WIDTH, QUERY_HEADS * HEAD_SIZE), (MODEL_WIDTH // 24) ** -0.5, 0.4375, ((1, 8),))
    key_weight = noise(keys[4], (MODEL_WIDTH, KEY_VALUE_HEADS * HEAD_SIZE), (MODEL_WIDTH // 6) ** -0.5, 0.21875, ((1, 8),))
    value_weight = noise(keys[5], (MODEL_WIDTH, KEY_VALUE_HEADS * HEAD_SIZE), (MODEL_WIDTH // 6) ** -0.5, 0.21875, ((1, 8),))
    w_out = noise(keys[6], (QUERY_HEADS * HEAD_SIZE, MODEL_WIDTH), (QUERY_HEADS * HEAD_SIZE) ** -0.5, 0.125, ((1, 8),))
    prefix_key_value_cache = noise(keys[7], (N_SEQ * PREFIX_LENGTH, 2, KEY_VALUE_HEADS * HEAD_SIZE), 2.5, 15.0, ((0, 32), (2, 8)))
    suffix_len = ragged(keys[8], REQS, SUFFIX_TOKENS, LONGEST_SUFFIX, 2).astype(jnp.int32)
    request_order = jax.random.permutation(keys[9], REQS).astype(jnp.int32)
    request_prefix = place_ends(jax.random.randint(keys[10], (REQS,), 0, NPRE), jax.random.fold_in(keys[10], 1), 0, NPRE - 1).astype(jnp.int32)
    prefix_owner = draw_prefix_owner(jax.random.fold_in(keys[12], 71), 0)
    return {"hidden_in": hidden_in, "pre_gain": pre_gain, "post_gain": post_gain, "w_query": w_query, "key_weight": key_weight, "value_weight": value_weight, "w_out": w_out, "prefix_key_value_cache": prefix_key_value_cache, "suffix_len": suffix_len, "request_order": request_order, "request_prefix": request_prefix, "prefix_owner": prefix_owner}


softcap = 50.0
rope_base = 10000.0
eps = 1e-06

def request_layout(suffix_len, request_order, request_prefix, token_ids):
    req_count = request_order.shape[0]
    ladder = jnp.arange(req_count, dtype=jnp.int32)
    chosen = (request_order[:, None] == ladder[None, :]).astype(jnp.int32)
    ordered_len = lax.optimization_barrier(jnp.sum(chosen * suffix_len[None, :], axis=1)).astype(jnp.int32)
    ordered_prefix = lax.optimization_barrier(jnp.sum(chosen * request_prefix[None, :], axis=1)).astype(jnp.int32)
    stop_at = jnp.cumsum(ordered_len).astype(jnp.int32)
    starts = (stop_at - ordered_len).astype(jnp.int32)
    slot_ids = lax.optimization_barrier(jnp.sum((stop_at[None, :] <= token_ids[:, None]).astype(jnp.int32), axis=1)).astype(jnp.int32)
    member = (slot_ids[:, None] == ladder[None, :]).astype(jnp.int32)
    positions = (token_ids - lax.optimization_barrier(jnp.sum(member * starts[None, :], axis=1))).astype(jnp.int32)
    prefixes = lax.optimization_barrier(jnp.sum(member * ordered_prefix[None, :], axis=1)).astype(jnp.int32)
    return (slot_ids, positions, prefixes)

def apply_rotary(value_rows, positions):
    half_width = value_rows.shape[-1] // 2
    ladder = jnp.arange(half_width, dtype=jnp.float32)
    frequency = rope_base ** (-2.0 * ladder / value_rows.shape[-1])
    angles = positions.astype(jnp.float32)[:, None] * frequency[None, :]
    cosine = jnp.cos(angles)[:, None, :]
    sine_part = jnp.sin(angles)[:, None, :]
    first_half = value_rows[..., :half_width]
    second_half = value_rows[..., half_width:]
    return jnp.concatenate([first_half * cosine - second_half * sine_part, second_half * cosine + first_half * sine_part], axis=-1)

def attend(query_rows, key_rows, value_rows, allowed):
    scores = jnp.einsum('tkgd,skd->tkgs', query_rows.astype(jnp.float32), key_rows.astype(jnp.float32)) * QSCALE ** (-0.5)
    capped = softcap * jnp.tanh(scores / softcap)
    weights = jnp.where(allowed[:, None, None, :], jnp.exp(capped), 0.0).astype(jnp.bfloat16)
    numerator = jnp.einsum('tkgs,skd->tkgd', weights.astype(jnp.float32), value_rows.astype(jnp.float32))
    softmax_denominator = lax.optimization_barrier(jnp.sum(weights.astype(jnp.float32), axis=-1))
    return (numerator, softmax_denominator)

def reference(hidden_in, pre_gain, post_gain, w_query, key_weight, value_weight, w_out, prefix_key_value_cache, suffix_len, request_order, request_prefix, prefix_owner):
    query_group = QUERY_HEADS // KEY_VALUE_HEADS
    token_ids = jnp.arange(SUFFIX_TOKENS, dtype=jnp.int32)
    slot_ids, positions, prefixes = request_layout(suffix_len, request_order, request_prefix, token_ids)
    wide = hidden_in.astype(jnp.float32)
    normed_input = (wide * lax.rsqrt(lax.optimization_barrier(jnp.mean(wide * wide, axis=1, keepdims=True)) + eps) * pre_gain[None, :]).astype(jnp.bfloat16)
    rotary_position = positions + PREFIX_LENGTH
    query_rows = jnp.dot(normed_input, w_query, preferred_element_type=jnp.float32).reshape(SUFFIX_TOKENS, QUERY_HEADS, HEAD_SIZE)
    query_rows = apply_rotary(query_rows, rotary_position).astype(jnp.bfloat16).reshape(SUFFIX_TOKENS, KEY_VALUE_HEADS, query_group, HEAD_SIZE)
    key_rows = jnp.dot(normed_input, key_weight, preferred_element_type=jnp.float32).reshape(SUFFIX_TOKENS, KEY_VALUE_HEADS, HEAD_SIZE)
    key_rows = apply_rotary(key_rows, rotary_position).astype(jnp.bfloat16)
    value_rows = jnp.dot(normed_input, value_weight, preferred_element_type=jnp.float32).astype(jnp.bfloat16).reshape(SUFFIX_TOKENS, KEY_VALUE_HEADS, HEAD_SIZE)
    cached_row_span = prefix_key_value_cache.reshape(N_SEQ, PREFIX_LENGTH, 2, KEY_VALUE_HEADS, HEAD_SIZE)
    used = jnp.take(cached_row_span, prefix_owner, axis=0)
    padded_keys = jnp.concatenate([jnp.zeros((LONGEST_SUFFIX, KEY_VALUE_HEADS, HEAD_SIZE), key_rows.dtype), key_rows], axis=0)
    padded_values = jnp.concatenate([jnp.zeros((LONGEST_SUFFIX, KEY_VALUE_HEADS, HEAD_SIZE), value_rows.dtype), value_rows], axis=0)
    slot_pad = jnp.concatenate([jnp.full((LONGEST_SUFFIX,), -1, dtype=jnp.int32), slot_ids], axis=0)
    block_row_count = TOK_DEV

    def one_block(start):
        query_blk = lax.dynamic_slice_in_dim(query_rows, start, block_row_count, 0)
        query_ids = start + jnp.arange(block_row_count, dtype=jnp.int32)
        query_slot = lax.dynamic_slice_in_dim(slot_ids, start, block_row_count, 0)
        query_prefix = lax.dynamic_slice_in_dim(prefixes, start, block_row_count, 0)
        numerator = jnp.zeros((block_row_count, KEY_VALUE_HEADS, query_group, HEAD_SIZE), jnp.float32)
        softmax_denominator = jnp.zeros((block_row_count, KEY_VALUE_HEADS, query_group), jnp.float32)
        for prefix_idx in range(NPRE):
            rows = (query_prefix == prefix_idx)[:, None]
            part_numer, part_total = attend(query_blk, used[prefix_idx, :, 0], used[prefix_idx, :, 1], rows)
            numerator = numerator + part_numer
            softmax_denominator = softmax_denominator + part_total
        key_blk = lax.dynamic_slice_in_dim(padded_keys, start, block_row_count + LONGEST_SUFFIX, 0)
        value_blk = lax.dynamic_slice_in_dim(padded_values, start, block_row_count + LONGEST_SUFFIX, 0)
        key_slot = lax.dynamic_slice_in_dim(slot_pad, start, block_row_count + LONGEST_SUFFIX, 0)
        key_ids = start - LONGEST_SUFFIX + jnp.arange(block_row_count + LONGEST_SUFFIX, dtype=jnp.int32)
        allowed = (key_ids[None, :] >= 0) & (key_ids[None, :] <= query_ids[:, None]) & (key_slot[None, :] == query_slot[:, None])
        part_numer, part_total = attend(query_blk, key_blk, value_blk, allowed)
        numerator = numerator + part_numer
        softmax_denominator = softmax_denominator + part_total
        return (numerator / softmax_denominator[..., None]).astype(jnp.bfloat16)
    starts = jnp.arange(SUFFIX_TOKENS // block_row_count, dtype=jnp.int32) * block_row_count
    attended = lax.map(one_block, starts).reshape(SUFFIX_TOKENS, QUERY_HEADS * HEAD_SIZE)
    projected = jnp.dot(attended, w_out, preferred_element_type=jnp.float32)
    post = projected * lax.rsqrt(lax.optimization_barrier(jnp.mean(projected * projected, axis=1, keepdims=True)) + eps) * post_gain[None, :]
    return (wide + post).astype(jnp.bfloat16)
```

```python
import math

import jax
import jax.numpy as jnp
import numpy as np
from jax import lax
from jax.experimental import pallas as pl
from jax.experimental.pallas import tpu as pltpu
from jax.sharding import PartitionSpec as P

MESH = pl.DeviceIdType.MESH
WIDTH = 4608
HEAD = 128
QSCALE = 144
PREFIX = 2048
TOK = 512
REQS = 48
SHARD = 576
PIECES = (("P", "R"), ("P", "L"), ("Q", "R"), ("Q", "L"))
SOFTCAP = 50.0
EPS = 1e-6
F32 = jnp.float32
BF16 = jnp.bfloat16


def remote(src, dst, ssem, rsem, where):
    return pltpu.make_async_remote_copy(
        src_ref=src, dst_ref=dst, send_sem=ssem, recv_sem=rsem, device_id=where, device_id_type=MESH
    )


class Gather:
    def __init__(self, own, buf, ssem, rsem, rows, x, l):
        self.own, self.buf, self.ssem, self.rsem, self.rows = own, buf, ssem, rsem, rows
        self.x, self.l = x, l
        self.count = 0
        self.started = []
        self.n = len(PIECES)
        self.prow = rows // self.n

    def target(self, way):
        x, l = self.x, self.l
        if way == "R":
            return {"tp": l * 4 + (x + 1) % 4}
        if way == "L":
            return {"tp": l * 4 + (x + 3) % 4}
        return {"tp": (1 - l) * 4 + x}

    def place(self, dx, dl, k):
        shard = ((self.l + dl) % 2) * 4 + (self.x + dx) % 4
        return self.buf.at[pl.ds(pl.multiple_of(shard * self.rows + k * self.prow, 16), self.prow)]

    def send(self, dx, dl, k, way):
        src = self.place(dx, dl, k)
        if dx == 0 and dl == 0:
            src = self.own.at[pl.ds(k * self.prow, self.prow)]
        rdx, rdl = dx, dl
        if way == "R":
            rdx = (dx + 3) % 4
        elif way == "L":
            rdx = (dx + 1) % 4
        else:
            rdl = 1 - dl
        copy = remote(
            src, self.place(dx, dl, k), self.ssem.at[self.count], self.rsem.at[(rdl * 4 + rdx) * self.n + k], self.target(way)
        )
        copy.start()
        self.count += 1
        self.started.append(copy)

    def wait(self, dx, dl, k):
        here = self.place(dx, dl, k)
        remote(here, here, self.ssem.at[0], self.rsem.at[(dl * 4 + dx) * self.n + k], self.target("R")).wait_recv()

    def start(self):
        for k in range(self.n):
            for way in ("R", "L", "Z"):
                self.send(0, 0, k, way)

    def first(self, k):
        kind, way = PIECES[k]
        self.wait(3, 0, k)
        if way == "R":
            self.send(3, 0, k, "R")
        if kind == "Q":
            self.send(3, 0, k, "Z")
        self.wait(1, 0, k)
        if way == "L":
            self.send(1, 0, k, "L")
        if kind == "Q":
            self.send(1, 0, k, "Z")
        self.wait(0, 1, k)
        if kind == "P":
            self.send(0, 1, k, "R")
            self.send(0, 1, k, "L")

    def second(self, k):
        kind, way = PIECES[k]
        self.wait(2, 0, k)
        if kind == "Q":
            self.send(2, 0, k, "Z")
        self.wait(3, 1, k)
        if kind == "P" and way == "R":
            self.send(3, 1, k, "R")
        self.wait(1, 1, k)
        if kind == "P" and way == "L":
            self.send(1, 1, k, "L")

    def third(self, k):
        self.wait(2, 1, k)

    def drain(self):
        for copy in self.started:
            copy.wait_send()


def gather_sends():
    total = 0
    for kind, _ in PIECES:
        total += 3 + 1 + (3 if kind == "Q" else 3)
    return total


def slot_tables(len_row, order_row, prefix_row):
    a = lax.broadcasted_iota(jnp.int32, (REQS, REQS), 0)
    b = lax.broadcasted_iota(jnp.int32, (REQS, REQS), 1)
    order_col = jnp.sum(jnp.where(a == b, jnp.broadcast_to(order_row, (REQS, REQS)), 0.0), axis=1, keepdims=True)
    chosen = order_col == b.astype(F32)
    length = jnp.sum(jnp.where(chosen, jnp.broadcast_to(len_row, (REQS, REQS)), 0.0), axis=1, keepdims=True)
    prefix = jnp.sum(jnp.where(chosen, jnp.broadcast_to(prefix_row, (REQS, REQS)), 0.0), axis=1, keepdims=True)
    length_row = jnp.sum(jnp.where(a == b, jnp.broadcast_to(length, (REQS, REQS)), 0.0), axis=0, keepdims=True)
    stop = jnp.sum(jnp.where(b <= a, jnp.broadcast_to(length_row, (REQS, REQS)), 0.0), axis=1, keepdims=True)
    return stop - length, stop, prefix


def kernel_in(
    owner_ref, len_ref, order_ref, pref_ref, gain_ref, freq_ref,
    h_hbm, wq_hbm, wk_hbm, wv_hbm, ck_ref, cv_ref,
    q_out, kv_out, f_out,
    h_buf, w_buf, wt, acc, sq, cos_buf, sin_buf, cache_f,
    y0, y1, s0, s1, c0, c1, z0, z1, p0, p1, kv_own,
    g_ssem, g_rsem, y_ssem, y_rsem, b_ssem, b_rsem, z_ssem, z_rsem, t_ssem, t_rsem,
    a_ssem, a_rsem, r_ssem, r_rsem, k_ssem, k_rsem, local_sem,
):
    s = lax.axis_index("seq")
    t = lax.axis_index("tp")
    zh, y, c = s // 8, (s // 2) % 4, s % 2
    l, x = t // 4, t % 4
    other = 1 - c
    sibling = {"seq": zh * 8 + y * 2 + other}

    def at_y(d):
        return {"seq": zh * 8 + ((y + d) % 4) * 2 + c}

    def at_z(d):
        return {"seq": ((zh + d) % 4) * 8 + y * 2 + c}

    ahead = {"seq": (s + 2) % 32}
    behind = {"seq": (s + 30) % 32}
    gather = Gather(h_hbm, h_buf, g_ssem, g_rsem, SHARD, x, l)

    barrier = pltpu.get_barrier_semaphore()
    peers = [gather.target("R"), gather.target("L"), gather.target("Z"), sibling, ahead, behind]
    peers += [at_y(1), at_y(2), at_y(3), at_z(1), at_z(2), at_z(3)]
    for peer in peers:
        pl.semaphore_signal(barrier, inc=1, device_id=peer, device_id_type=MESH)

    local = []

    def copy_here(src, dst):
        cp = pltpu.make_async_copy(src, dst, local_sem.at[len(local)])
        cp.start()
        local.append(cp)
        return cp

    weights = [
        copy_here(wq_hbm, w_buf.at[:, pl.ds(0, 256)]),
        copy_here(wk_hbm, w_buf.at[:, pl.ds(256, 128)]),
        copy_here(wv_hbm, w_buf.at[:, pl.ds(384, 128)]),
        copy_here(h_hbm, h_buf.at[pl.ds(pl.multiple_of(t * SHARD, 16), SHARD)]),
    ]
    pl.semaphore_wait(barrier, len(peers))
    gather.start()

    @pl.loop(0, 16)
    def _(b):
        rows = pl.ds(pl.multiple_of(b * 128, 128), 128)
        cache_f[b, 0:128, :] = ck_ref[rows, :]
        cache_f[b, 128:256, :] = cv_ref[rows, :].astype(F32).T.astype(BF16)

    halves = ((y0, s0, c0, z0, p0), (y1, s1, c1, z1, p1))
    pending = []

    def push(src, dst, ssem, rsem, where):
        cp = remote(src, dst, ssem, rsem, where)
        cp.start()
        pending.append(cp)

    def landed(ref, rsem):
        remote(ref, ref, y_ssem.at[0], rsem, sibling).wait_recv()

    own_y = []
    for h in range(2):
        yb = halves[h][0]
        for d in (1, 3, 2):
            j = (y + d) % 4
            push(cache_f.at[pl.ds(j * 4 + h * 2, 2)], yb.at[y], y_ssem.at[h * 3 + d - 1], y_rsem.at[h * 3 + 3 - d], at_y(d))
        own_y.append(copy_here(cache_f.at[pl.ds(y * 4 + h * 2, 2)], yb.at[y]))

    oc = jnp.int32(-1)
    od = jnp.int32(-1)
    for p in range(4):
        o = owner_ref[p]
        inner = jnp.logical_and(o != 0, o != 31)
        fresh = oc < 0
        od = jnp.where(jnp.logical_and(inner, jnp.logical_not(fresh)), o, od)
        oc = jnp.where(jnp.logical_and(inner, fresh), o, oc)
    oc = jnp.clip(oc, 0, 31)
    od = jnp.clip(od, 0, 31)
    mine = jnp.where(c == 0, oc, od)
    theirs = jnp.where(c == 0, od, oc)

    def quarter(item, j, h):
        return f_out.at[item, pl.ds(j * 4 + h * 2, 2)]

    is_end = zh == 3 * c

    def stage_y(h):
        yb, sb, cb, zb, pb = halves[h]
        own_y[h].wait()
        for d in (1, 3, 2):
            landed(yb.at[(y + d) % 4], y_rsem.at[h * 3 + d - 1])
        sb[...] = yb[(theirs >> 1) & 3]
        push(sb, cb.at[c], b_ssem.at[h], b_rsem.at[h], sibling)

        @pl.when(is_end)
        def _():
            for d in (1, 3, 2):
                remote(yb.at[3 * c], quarter(c, y, h), a_ssem.at[h * 4 + d], a_rsem.at[h], at_z(d)).start()
            pltpu.make_async_copy(yb.at[3 * c], quarter(c, y, h), a_ssem.at[h * 4]).start()

        cb[c] = yb[(mine >> 1) & 3]

    def stage_core(h):
        yb, sb, cb, zb, pb = halves[h]
        landed(cb.at[other], b_rsem.at[h])
        zb[zh] = cb[mine & 1]
        for d in (1, 3, 2):
            push(zb.at[zh], zb.at[zh], z_ssem.at[h * 3 + d - 1], z_rsem.at[h * 3 + 3 - d], at_z(d))

    def relay(item, j, h, i, d):
        n = (i * 4 + d) * 2 + h
        push(quarter(item, j, h), quarter(item, j, h), r_ssem.at[n], r_rsem.at[n], sibling)

    def stage_z(h):
        yb, sb, cb, zb, pb = halves[h]
        for d in (1, 3, 2):
            landed(zb.at[(zh + d) % 4], z_rsem.at[h * 3 + d - 1])

        @pl.when(jnp.logical_not(is_end))
        def _():
            landed(quarter(c, y, h), a_rsem.at[h])

        @pl.when(is_end)
        def _():
            pltpu.make_async_copy(yb.at[3 * c], quarter(c, y, h), a_ssem.at[h * 4]).wait()

        pb[...] = zb[mine >> 3]
        copy_here(pb, quarter(c + 2, y, h))
        for i, src in ((0, quarter(c, y, h)), (1, pb)):
            item = c + 2 * i
            for d in (1, 3):
                push(src, quarter(item, y, h), t_ssem.at[(i * 3 + d - 1) * 2 + h], t_rsem.at[(i * 3 + 3 - d) * 2 + h], at_y(d))
            n = (i * 4) * 2 + h
            push(src, quarter(item, y, h), r_ssem.at[n], r_rsem.at[n], sibling)

    def stage_spread(h):
        for i in range(2):
            item = c + 2 * i
            for d in (3, 1):
                j = (y + d) % 4
                landed(quarter(item, j, h), t_rsem.at[(i * 3 + d - 1) * 2 + h])
                if (i == 0 and d == 3) or (i == 1 and d == 1):
                    push(
                        quarter(item, j, h), quarter(item, j, h), t_ssem.at[(i * 3 + 1) * 2 + h], t_rsem.at[(i * 3 + 1) * 2 + h],
                        at_y(1 if i == 0 else 3),
                    )
                relay(item, j, h, i, d)

    def stage_far(h):
        for i in range(2):
            item = c + 2 * i
            j = (y + 2) % 4
            landed(quarter(item, j, h), t_rsem.at[(i * 3 + 1) * 2 + h])
            relay(item, j, h, i, 2)

    def rotary_tables():
        first, stop, _ = slot_tables(len_ref[...], order_ref[...], pref_ref[...])
        tok = (lax.broadcasted_iota(jnp.int32, (1, TOK), 1) + s * TOK).astype(F32)
        start = jnp.max(jnp.where(stop <= tok, jnp.broadcast_to(stop, (REQS, TOK)), 0.0), axis=0, keepdims=True)
        place = tok - start + float(PREFIX)
        angle = freq_ref[...] * place
        cos_buf[...] = jnp.cos(angle)
        sin_buf[...] = jnp.sin(angle)

    def turn_weights(i):
        @pl.loop(i * 9, i * 9 + 9)
        def _(f):
            rows = pl.ds(pl.multiple_of(f * 128, 128), 128)
            g = gain_ref[pl.ds(f, 1), :]
            for cb in range(4):
                w = w_buf[rows, cb * 128:(cb + 1) * 128].astype(F32).T
                wt[cb * 128:(cb + 1) * 128, rows] = (w * g).astype(BF16)

    def multiply(pair, begin):
        rows = pl.multiple_of(pair * 1152, 128)

        @pl.loop(0, 2)
        def _(m):
            mm = pl.ds(pl.multiple_of(m * 256, 256), 256)
            part = jnp.dot(wt[mm, pl.ds(rows, 1152)], h_buf[pl.ds(rows, 1152), :], preferred_element_type=F32)
            acc[mm, :] = part if begin else acc[mm, :] + part

        @pl.loop(0, 9)
        def _(b):
            v = h_buf[pl.ds(pl.multiple_of(rows + b * 128, 128), 128), :].astype(F32)
            v = v * v
            tot = v[0:8]
            for e in range(1, 16):
                tot = tot + v[e * 8:(e + 1) * 8]
            sq[...] = sq[...] + tot

    sq[...] = jnp.zeros_like(sq)
    for cp in weights:
        cp.wait()
    turn_weights(0)
    gather.first(0)
    stage_y(0)
    stage_core(0)
    turn_weights(1)
    gather.first(1)
    turn_weights(2)
    gather.first(2)
    stage_y(1)
    stage_core(1)
    turn_weights(3)
    gather.first(3)
    near = l * 2 + x // 2
    multiply(near, True)
    rotary_tables()
    gather.second(0)
    stage_z(0)
    gather.second(1)
    gather.second(2)
    gather.second(3)
    multiply(l * 2 + 1 - x // 2, False)
    stage_z(1)
    multiply((1 - l) * 2 + x // 2, False)
    stage_spread(0)
    for k in range(4):
        gather.third(k)
    multiply((1 - l) * 2 + 1 - x // 2, False)

    scale = lax.rsqrt(jnp.sum(sq[...], axis=0, keepdims=True) * (1.0 / WIDTH) + EPS)
    cos, sin = cos_buf[...], sin_buf[...]

    def turned(r0):
        a = acc[r0:r0 + 64, :] * scale
        b = acc[r0 + 64:r0 + 128, :] * scale
        return a * cos - b * sin, b * cos + a * sin

    a, b = turned(256)
    kt = jnp.concatenate([a, b], axis=0)
    vt = (acc[384:512, :] * scale).astype(BF16)
    for blk in range(4):
        kv_own[blk, 0:128, :] = kt[:, blk * 128:(blk + 1) * 128].T.astype(BF16)
        kv_own[blk, 128:256, :] = vt[:, blk * 128:(blk + 1) * 128]

    def kv(slot, g):
        return kv_out.at[slot, pl.ds(g * 2, 2)]

    sib_slot = (5 - 2 * other, 3 - 2 * other, 1 + 4 * other)
    my_slot = (5 - 2 * c, 3 - 2 * c, 1 + 4 * c)
    for g in range(2):
        src = kv_own.at[pl.ds(g * 2, 2)]
        push(src, kv(2, g), k_ssem.at[g], k_rsem.at[g], ahead)
    for g in range(2):
        src = kv_own.at[pl.ds(g * 2, 2)]
        push(src, kv(sib_slot[0], g), k_ssem.at[4 + g], k_rsem.at[4 + g], sibling)
    copy_here(kv_own, kv_out.at[4])
    for hd in range(2):
        a, b = turned(hd * 128)
        q_out[hd * 128:hd * 128 + 64, :] = a.astype(BF16)
        q_out[hd * 128 + 64:hd * 128 + 128, :] = b.astype(BF16)
    stage_spread(1)
    stage_far(0)
    for g in range(2):
        landed(kv(2, g), k_rsem.at[g])
        push(kv(2, g), kv(0, g), k_ssem.at[2 + g], k_rsem.at[2 + g], ahead)
        push(kv(2, g), kv(sib_slot[1], g), k_ssem.at[6 + g], k_rsem.at[6 + g], sibling)
    stage_far(1)
    for g in range(2):
        landed(kv(0, g), k_rsem.at[2 + g])
        push(kv(0, g), kv(sib_slot[2], g), k_ssem.at[8 + g], k_rsem.at[8 + g], sibling)
    for i in range(2):
        item = other + 2 * i
        for d in range(4):
            for h in range(2):
                landed(quarter(item, (y + d) % 4, h), r_rsem.at[(i * 4 + d) * 2 + h])
    for n in range(3):
        for g in range(2):
            landed(kv(my_slot[n], g), k_rsem.at[4 + 2 * n + g])
    gather.drain()
    for cp in pending:
        cp.wait_send()
    for h in range(2):
        @pl.when(is_end)
        def _():
            for d in (1, 3, 2):
                remote(halves[h][0].at[3 * c], quarter(c, y, h), a_ssem.at[h * 4 + d], a_rsem.at[h], at_z(d)).wait_send()
    for cp in local[4 + 2:]:
        cp.wait()


def kernel_attend(
    owner_s, len_s, order_s, pref_s, base_s, len_ref, order_ref, pref_ref, q_ref, kv_hbm, f_hbm,
    out_ref, kv_buf, f_buf, acc, kv_sem, f_sem,
):
    kv_copy = pltpu.make_async_copy(kv_hbm.at[pl.ds(0, 5)], kv_buf, kv_sem)
    kv_copy.start()
    base = base_s[0]
    items = []
    seen = jnp.int32(0)
    for p in range(4):
        o = owner_s[p]
        inner = jnp.logical_and(o != 0, o != 31)
        items.append(jnp.where(o == 0, 0, jnp.where(o == 31, 1, 2 + seen)))
        seen = seen + inner.astype(jnp.int32)

    def look(r, carry):
        at = carry[0]
        req = order_s[r]
        stop = at + len_s[req]
        bit = jnp.int32(1) << pref_s[req]
        out = [stop]
        for rb in range(4):
            lo = base + rb * 128
            hit = jnp.logical_and(at < lo + 128, stop > lo)
            out.append(jnp.where(hit, carry[1 + 2 * rb] | bit, carry[1 + 2 * rb]))
            out.append(jnp.where(jnp.logical_and(at <= lo, stop > lo), at, carry[2 + 2 * rb]))
        return tuple(out)

    zero = jnp.int32(0)
    found = lax.fori_loop(0, REQS, look, (zero,) * 9)
    flags = [found[1 + 2 * rb] for rb in range(4)]
    begins = [found[2 + 2 * rb] for rb in range(4)]
    every = flags[0] | flags[1] | flags[2] | flags[3]
    for p in range(4):
        @pl.when(((every >> p) & 1) == 1)
        def _():
            pltpu.make_async_copy(f_hbm.at[items[p]], f_buf.at[p], f_sem.at[p]).start()

    first, stop, prefix = slot_tables(len_ref[...], order_ref[...], pref_ref[...])
    c1 = float(QSCALE ** -0.5 / SOFTCAP)
    c2 = float(SOFTCAP * math.log2(math.e))
    ones = jnp.ones((16, 256), BF16)
    kv_copy.wait()

    def weigh(k2, qt):
        sc = jnp.dot(k2, qt, preferred_element_type=F32)
        return jnp.exp2(jnp.tanh(sc * c1) * c2)

    for rb in range(4):
        lanes = pl.ds(rb * 128, 128)
        qt = jnp.concatenate([q_ref[0:128, lanes], q_ref[128:256, lanes]], axis=1)
        tok = (lax.broadcasted_iota(jnp.int32, (1, 256), 1) % 128 + (base + rb * 128)).astype(F32)
        begin = jnp.max(jnp.where(stop <= tok, jnp.broadcast_to(stop, (REQS, 256)), 0.0), axis=0, keepdims=True)
        inside = jnp.logical_and(first <= tok, tok < stop)
        pref = jnp.sum(jnp.where(inside, jnp.broadcast_to(prefix, (REQS, 256)), 0.0), axis=0, keepdims=True)
        acc[...] = jnp.zeros_like(acc)
        origin = base - 2048
        low = (begins[rb] - origin) // 256

        @pl.loop(low, (2048 + rb * 128 + 128 + 255) // 256)
        def _(n):
            slot, blk = n // 2, (n % 2) * 2
            k2 = jnp.concatenate([kv_buf[slot, blk, 0:128, :], kv_buf[slot, blk + 1, 0:128, :]], axis=0)
            v2 = jnp.concatenate([kv_buf[slot, blk, 128:256, :], kv_buf[slot, blk + 1, 128:256, :]], axis=1)
            key = (lax.broadcasted_iota(jnp.int32, (256, 1), 0) + (origin + n * 256)).astype(F32)
            ok = jnp.logical_and(key <= tok, key >= begin)
            w = jnp.where(ok, weigh(k2, qt), 0.0).astype(BF16)
            acc[...] += jnp.dot(jnp.concatenate([v2, ones], axis=0), w, preferred_element_type=F32)

        for p in range(4):
            @pl.when(((flags[rb] >> p) & 1) == 1)
            def _():
                @pl.when(((every >> p) & 1) == 1)
                def _():
                    earlier = jnp.int32(0)
                    for q in range(rb):
                        earlier = earlier | flags[q]

                    @pl.when(((earlier >> p) & 1) == 0)
                    def _():
                        pltpu.make_async_copy(f_hbm.at[0], f_buf.at[p], f_sem.at[p]).wait()

                rowmask = pref == float(p)

                @pl.loop(0, 8)
                def _(n):
                    blk = n * 2
                    k2 = jnp.concatenate([f_buf[p, blk, 0:128, :], f_buf[p, blk + 1, 0:128, :]], axis=0)
                    v2 = jnp.concatenate([f_buf[p, blk, 128:256, :], f_buf[p, blk + 1, 128:256, :]], axis=1)
                    w = weigh(k2, qt).astype(BF16)
                    part = jnp.dot(jnp.concatenate([v2, ones], axis=0), w, preferred_element_type=F32)
                    acc[...] += jnp.where(rowmask, part, 0.0)

        att = acc[0:128, :] / acc[128:129, :]
        out_ref[0:128, lanes] = att[:, 0:128].astype(BF16)
        out_ref[128:256, lanes] = att[:, 128:256].astype(BF16)


def kernel_out(
    att_ref, wo_hbm, h_ref, gain_ref, out_ref, g_buf, wo_buf, acc, gcol, sums, g_ssem, g_rsem, q_ssem, q_rsem, local_sem
):
    s = lax.axis_index("seq")
    t = lax.axis_index("tp")
    l, x = t // 4, t % 4
    gather = Gather(att_ref, g_buf, g_ssem, g_rsem, 256, x, l)

    def peer(d):
        return {"tp": (t + d) % 8}

    barrier = pltpu.get_barrier_semaphore()
    for d in range(1, 8):
        pl.semaphore_signal(barrier, inc=1, device_id=peer(d), device_id_type=MESH)
    wo_copy = pltpu.make_async_copy(wo_hbm, wo_buf, local_sem.at[0])
    own_copy = pltpu.make_async_copy(att_ref, g_buf.at[pl.ds(pl.multiple_of(t * 256, 256), 256)], local_sem.at[1])
    wo_copy.start()
    own_copy.start()
    pl.semaphore_wait(barrier, 7)
    gather.start()

    g5 = gain_ref[t]
    for b in range(5):
        gcol[b * 128:(b + 1) * 128, :] = jnp.broadcast_to(g5[b:b + 1, :], (128, 128)).T
    wo_copy.wait()
    own_copy.wait()

    def multiply(dx, dl, begin):
        shard = ((l + dl) % 2) * 4 + (x + dx) % 4
        rows = pl.ds(pl.multiple_of(shard * 256, 256), 256)

        @pl.loop(0, 4)
        def _(m):
            mm = pl.ds(pl.multiple_of(m * 144, 16), 144)
            part = jnp.dot(wo_buf[mm, rows], g_buf[rows, :], preferred_element_type=F32)
            acc[mm, :] = part if begin else acc[mm, :] + part

    multiply(0, 0, True)
    for k in range(4):
        gather.first(k)
    multiply(1, 0, False)
    multiply(3, 0, False)
    multiply(0, 1, False)
    for k in range(4):
        gather.second(k)
    multiply(2, 0, False)
    multiply(1, 1, False)
    multiply(3, 1, False)
    for k in range(4):
        gather.third(k)
    multiply(2, 1, False)

    tot = jnp.zeros((8, TOK), F32)
    for b in range(72):
        v = acc[b * 8:(b + 1) * 8, :]
        tot = tot + v * v
    sums[t] = tot
    copies = []
    for d in range(1, 8):
        cp = remote(sums.at[t], sums.at[t], q_ssem.at[d - 1], q_rsem.at[7 - d], peer(d))
        cp.start()
        copies.append(cp)
    for d in range(1, 8):
        here = sums.at[(t + d) % 8]
        remote(here, here, q_ssem.at[0], q_rsem.at[d - 1], peer(1)).wait_recv()
    tot = sums[0]
    for d in range(1, 8):
        tot = tot + sums[d]
    scale = lax.rsqrt(jnp.sum(tot, axis=0, keepdims=True) * (1.0 / WIDTH) + EPS)
    for b in range(9):
        rows = slice(b * 64, b * 64 + 64)
        g = gcol[rows, :]
        for n in range(4):
            cols = slice(n * 128, n * 128 + 128)
            post = acc[rows, cols] * scale[:, cols] * g
            out_ref[rows, cols] = (h_ref[rows, cols].astype(F32) + post).astype(BF16)
    gather.drain()
    for cp in copies:
        cp.wait_send()


def on_device(
    hidden_in, pre_gain, post_gain, w_query, key_weight, value_weight, w_out, cache, suffix_len, request_order,
    request_prefix, prefix_owner,
):
    any_spec = pl.BlockSpec(memory_space=pl.ANY)
    vmem = pl.BlockSpec(memory_space=pltpu.VMEM)
    smem = pl.BlockSpec(memory_space=pltpu.SMEM)
    dma = pltpu.SemaphoreType.DMA
    h_t = hidden_in.T
    len_row = suffix_len.astype(F32).reshape(1, REQS)
    order_row = request_order.astype(F32).reshape(1, REQS)
    pref_row = request_prefix.astype(F32).reshape(1, REQS)
    freq = jnp.asarray((10000.0 ** (-2.0 * np.arange(64) / HEAD)).astype(np.float32).reshape(64, 1))
    sends = gather_sends()
    n = len(PIECES)
    half = pltpu.VMEM((2, 256, 128), BF16)
    four = pltpu.VMEM((4, 2, 256, 128), BF16)
    two = pltpu.VMEM((2, 2, 256, 128), BF16)
    q, kv, spread = pl.pallas_call(
        kernel_in,
        out_shape=(
            jax.ShapeDtypeStruct((256, TOK), BF16),
            jax.ShapeDtypeStruct((6, 4, 256, 128), BF16),
            jax.ShapeDtypeStruct((4, 16, 256, 128), BF16),
        ),
        in_specs=[smem, vmem, vmem, vmem, vmem, vmem, any_spec, any_spec, any_spec, any_spec, vmem, vmem],
        out_specs=(vmem, any_spec, any_spec),
        scratch_shapes=[
            pltpu.VMEM((WIDTH, TOK), BF16),
            pltpu.VMEM((WIDTH, 512), BF16),
            pltpu.VMEM((512, WIDTH), BF16),
            pltpu.VMEM((512, TOK), F32),
            pltpu.VMEM((8, TOK), F32),
            pltpu.VMEM((64, TOK), F32),
            pltpu.VMEM((64, TOK), F32),
            pltpu.VMEM((16, 256, 128), BF16),
            four, four, half, half, two, two, four, four, half, half,
            pltpu.VMEM((4, 256, 128), BF16),
            dma((sends,)), dma((8 * n,)), dma((6,)), dma((6,)), dma((2,)), dma((2,)), dma((6,)), dma((6,)),
            dma((12,)), dma((12,)), dma((8,)), dma((2,)), dma((16,)), dma((16,)), dma((10,)), dma((10,)), dma((12,)),
        ],
        compiler_params=pltpu.CompilerParams(collective_id=0, has_side_effects=True, vmem_limit_bytes=60 << 20),
    )(
        prefix_owner, len_row, order_row, pref_row, pre_gain.reshape(36, 128), freq,
        h_t, w_query, key_weight, value_weight, cache[:, 0, :], cache[:, 1, :],
    )
    base = (lax.axis_index("seq") * TOK).astype(jnp.int32).reshape(1)
    att = pl.pallas_call(
        kernel_attend,
        out_shape=jax.ShapeDtypeStruct((256, TOK), BF16),
        in_specs=[smem] * 5 + [vmem] * 4 + [any_spec, any_spec],
        out_specs=vmem,
        scratch_shapes=[
            pltpu.VMEM((5, 4, 256, 128), BF16),
            pltpu.VMEM((4, 16, 256, 128), BF16),
            pltpu.VMEM((144, 256), F32),
            dma, dma((4,)),
        ],
        compiler_params=pltpu.CompilerParams(vmem_limit_bytes=32 << 20),
    )(prefix_owner, suffix_len, request_order, request_prefix, base, len_row, order_row, pref_row, q, kv, spread)
    gains = jnp.pad(post_gain.reshape(8, SHARD), ((0, 0), (0, 64))).reshape(8, 5, 128)
    out = pl.pallas_call(
        kernel_out,
        out_shape=jax.ShapeDtypeStruct((SHARD, TOK), BF16),
        in_specs=[vmem, any_spec, vmem, vmem],
        out_specs=vmem,
        scratch_shapes=[
            pltpu.VMEM((2048, TOK), BF16),
            pltpu.VMEM((SHARD, 2048), BF16),
            pltpu.VMEM((SHARD, TOK), F32),
            pltpu.VMEM((640, 128), F32),
            pltpu.VMEM((8, 8, TOK), F32),
            dma((sends,)), dma((8 * n,)), dma((7,)), dma((7,)), dma((2,)),
        ],
        compiler_params=pltpu.CompilerParams(collective_id=1, has_side_effects=True, vmem_limit_bytes=32 << 20),
    )(att, w_out.T, h_t, gains)
    return out.T


def solution(mesh):
    placed = (
        P("seq", "tp"), P(), P(), P(None, "tp"), P(None, "tp"), P(None, "tp"), P(None, "tp"), P("seq", None, "tp"),
        P(), P(), P(), P(),
    )
    return jax.shard_map(on_device, mesh=mesh, in_specs=placed, out_specs=P("seq", "tp"), check_vma=False)
```

```python
import math

import jax
import jax.numpy as jnp
import numpy as np
from jax import lax
from jax.experimental import pallas as pl
from jax.experimental.pallas import tpu as pltpu
from jax.sharding import PartitionSpec as P

MESH = pl.DeviceIdType.MESH
WIDTH = 4608
HEAD = 128
QSCALE = 144
PREFIX = 2048
TOK = 512
REQS = 48
SHARD = 576
IN_PIECES = (("P", "R"), ("P", "L"), ("P", "R"), ("P", "L"))
OUT_PIECES = (("P", "R"), ("P", "L"), ("Q", "R"), ("Q", "L"))
SOFTCAP = 50.0
EPS = 1e-6
KEYS = 512
ON = ("mm", "gather", "prefix", "kv")
SCHED = (
    ("W", 0), ("g1", 0), ("sy", 0), ("sc", 0), ("W", 1), ("g1", 1), ("sr", 0), ("W", 2), ("g1", 2),
    ("so", 0), ("sy", 1), ("sc", 1), ("W", 3), ("g1", 3), ("ss", 0), ("sr", 1), ("M", 0), ("rot", 0),
    ("g2", 0), ("se", 0), ("sz", 0), ("so", 1), ("g2", 1), ("g2", 2), ("ss", 1), ("sp", 0), ("g2", 3),
    ("M", 1), ("se", 1), ("sz", 1), ("M", 2), ("sf", 0), ("g3", 0), ("g3", 1), ("g3", 2), ("g3", 3),
    ("M", 3), ("fin", 0), ("kv", 0), ("q", 0), ("sp", 1), ("kt", 0), ("kt", 1), ("k1", 0), ("k1", 1),
    ("sf", 1), ("k2", 0), ("k2", 1),
)
F32 = jnp.float32
BF16 = jnp.bfloat16


def remote(src, dst, ssem, rsem, where):
    return pltpu.make_async_remote_copy(
        src_ref=src, dst_ref=dst, send_sem=ssem, recv_sem=rsem, device_id=where, device_id_type=MESH
    )


class Gather:
    def __init__(self, pieces, own, buf, ssem, rsem, rows, x, l):
        self.pieces = pieces
        self.own, self.buf, self.ssem, self.rsem, self.rows = own, buf, ssem, rsem, rows
        self.x, self.l = x, l
        self.count = 0
        self.started = []
        self.n = len(pieces)
        self.prow = rows // self.n

    def target(self, way):
        x, l = self.x, self.l
        if way == "R":
            return {"tp": l * 4 + (x + 1) % 4}
        if way == "L":
            return {"tp": l * 4 + (x + 3) % 4}
        return {"tp": (1 - l) * 4 + x}

    def place(self, dx, dl, k):
        shard = ((self.l + dl) % 2) * 4 + (self.x + dx) % 4
        return self.buf.at[pl.ds(pl.multiple_of(shard * self.rows + k * self.prow, 16), self.prow)]

    def send(self, dx, dl, k, way):
        src = self.place(dx, dl, k)
        if dx == 0 and dl == 0:
            src = self.own.at[pl.ds(k * self.prow, self.prow)]
        rdx, rdl = dx, dl
        if way == "R":
            rdx = (dx + 3) % 4
        elif way == "L":
            rdx = (dx + 1) % 4
        else:
            rdl = 1 - dl
        copy = remote(
            src, self.place(dx, dl, k), self.ssem.at[self.count], self.rsem.at[(rdl * 4 + rdx) * self.n + k], self.target(way)
        )
        copy.start()
        self.count += 1
        self.started.append(copy)

    def wait(self, dx, dl, k):
        here = self.place(dx, dl, k)
        remote(here, here, self.ssem.at[0], self.rsem.at[(dl * 4 + dx) * self.n + k], self.target("R")).wait_recv()

    def start(self):
        for k in range(self.n):
            for way in ("R", "L", "Z"):
                self.send(0, 0, k, way)

    def first(self, k):
        kind, way = self.pieces[k]
        self.wait(3, 0, k)
        if way == "R":
            self.send(3, 0, k, "R")
        if kind == "Q":
            self.send(3, 0, k, "Z")
        self.wait(1, 0, k)
        if way == "L":
            self.send(1, 0, k, "L")
        if kind == "Q":
            self.send(1, 0, k, "Z")
        self.wait(0, 1, k)
        if kind == "P":
            self.send(0, 1, k, "R")
            self.send(0, 1, k, "L")

    def second(self, k):
        kind, way = self.pieces[k]
        self.wait(2, 0, k)
        if kind == "Q":
            self.send(2, 0, k, "Z")
        self.wait(3, 1, k)
        if kind == "P" and way == "R":
            self.send(3, 1, k, "R")
        self.wait(1, 1, k)
        if kind == "P" and way == "L":
            self.send(1, 1, k, "L")

    def third(self, k):
        self.wait(2, 1, k)

    def drain(self):
        for copy in self.started:
            copy.wait_send()


def slot_tables(len_row, order_row, prefix_row):
    len_row, order_row, prefix_row = (v.astype(F32) for v in (len_row, order_row, prefix_row))
    a = lax.broadcasted_iota(jnp.int32, (REQS, REQS), 0)
    b = lax.broadcasted_iota(jnp.int32, (REQS, REQS), 1)
    order_col = jnp.sum(jnp.where(a == b, jnp.broadcast_to(order_row, (REQS, REQS)), 0.0), axis=1, keepdims=True)
    chosen = order_col == b.astype(F32)
    length = jnp.sum(jnp.where(chosen, jnp.broadcast_to(len_row, (REQS, REQS)), 0.0), axis=1, keepdims=True)
    prefix = jnp.sum(jnp.where(chosen, jnp.broadcast_to(prefix_row, (REQS, REQS)), 0.0), axis=1, keepdims=True)
    length_row = jnp.sum(jnp.where(a == b, jnp.broadcast_to(length, (REQS, REQS)), 0.0), axis=0, keepdims=True)
    stop = jnp.sum(jnp.where(b <= a, jnp.broadcast_to(length_row, (REQS, REQS)), 0.0), axis=1, keepdims=True)
    return stop - length, stop, prefix


def kernel_in(
    owner_ref, len_ref, order_ref, pref_ref, gain_ref, freq_ref,
    h_hbm, wq_hbm, wk_hbm, wv_hbm, cache_ref,
    q_out, kv_out, f_out,
    h_buf, w_buf, wt, acc, sq, cos_buf, sin_buf, cache_f,
    y0, y1, s0, s1, c0, c1, z0, z1, p0, p1, i0, i1, m0, m1, kv_own, kv_via,
    g_ssem, g_rsem, y_ssem, y_rsem, b_ssem, b_rsem, z_ssem, z_rsem, t_ssem, t_rsem,
    a_ssem, a_rsem, e_sem, r_ssem, r_rsem, k_ssem, k_rsem, local_sem,
):
    s = lax.axis_index("seq")
    t = lax.axis_index("tp")
    zh, y, c = s // 8, (s // 2) % 4, s % 2
    l, x = t // 4, t % 4
    other = 1 - c
    sibling = {"seq": zh * 8 + y * 2 + other}

    def at_y(d):
        return {"seq": zh * 8 + ((y + d) % 4) * 2 + c}

    def at_z(d):
        return {"seq": ((zh + d) % 4) * 8 + y * 2 + c}

    gather = Gather(IN_PIECES, h_hbm, h_buf, g_ssem, g_rsem, SHARD, x, l)

    barrier = pltpu.get_barrier_semaphore()
    peers = [gather.target("R"), gather.target("L"), gather.target("Z"), sibling]
    peers += [at_y(1), at_y(2), at_y(3), at_z(1), at_z(3)]
    for peer in peers:
        pl.semaphore_signal(barrier, inc=1, device_id=peer, device_id_type=MESH)

    local = []

    def copy_here(src, dst):
        cp = pltpu.make_async_copy(src, dst, local_sem.at[len(local)])
        cp.start()
        local.append(cp)
        return cp

    weights = [
        copy_here(wq_hbm, w_buf.at[:, pl.ds(0, 256)]),
        copy_here(wk_hbm, w_buf.at[:, pl.ds(256, 128)]),
        copy_here(wv_hbm, w_buf.at[:, pl.ds(384, 128)]),
        copy_here(h_hbm, h_buf.at[pl.ds(pl.multiple_of(t * SHARD, 16), SHARD)]),
    ]
    pl.semaphore_wait(barrier, len(peers))
    if "gather" in ON:
        gather.start()

    to = lax.broadcasted_iota(jnp.int32, (256, 256), 0)
    of = lax.broadcasted_iota(jnp.int32, (256, 256), 1)
    apart = jnp.where(of == 2 * to - jnp.where(to < 128, 0, 255), 1.0, 0.0).astype(BF16)

    def split_cache(b0, b1):
        @pl.loop(b0, b1)
        def _(b):
            rows = pl.ds(pl.multiple_of(b * 256, 256), 256)
            both = jnp.dot(apart, cache_ref[rows, :], preferred_element_type=F32)
            cache_f[b * 2] = both[0:128].astype(BF16)
            cache_f[b * 2 + 1] = both[128:256].T.astype(BF16)

    if "prefix" in ON:
        split_cache(0, 16)

    halves = ((y0, s0, c0, z0, p0), (y1, s1, c1, z1, p1))
    zin, zmid = (i0, i1), (m0, m1)
    pending = []

    def push(src, dst, ssem, rsem, where):
        cp = remote(src, dst, ssem, rsem, where)
        cp.start()
        pending.append(cp)

    def landed(ref, rsem):
        remote(ref, ref, y_ssem.at[0], rsem, sibling).wait_recv()

    own_y = []
    for h in (range(2) if "prefix" in ON else ()):
        yb = halves[h][0]
        for d in (1, 3, 2):
            j = (y + d) % 4
            push(cache_f.at[pl.ds(j * 8 + h * 4, 4)], yb.at[y], y_ssem.at[h * 3 + d - 1], y_rsem.at[h * 3 + 3 - d], at_y(d))
        own_y.append(copy_here(cache_f.at[pl.ds(y * 8 + h * 4, 4)], yb.at[y]))

    oc = jnp.int32(-1)
    od = jnp.int32(-1)
    for p in range(4):
        o = owner_ref[p]
        inner = jnp.logical_and(o != 0, o != 31)
        fresh = oc < 0
        od = jnp.where(jnp.logical_and(inner, jnp.logical_not(fresh)), o, od)
        oc = jnp.where(jnp.logical_and(inner, fresh), o, oc)
    oc = jnp.clip(oc, 0, 31)
    od = jnp.clip(od, 0, 31)
    mine = jnp.where(c == 0, oc, od)
    theirs = jnp.where(c == 0, od, oc)

    def quarter(item, j, h):
        return f_out.at[item, pl.ds(j * 8 + h * 4, 4)]

    far = (zh - 3 * c) % 4

    def end_copy(h, d, src):
        return remote(src, quarter(c, y, h), a_ssem.at[h * 2 + d // 2], a_rsem.at[h], at_z(d))

    def stage_y(h):
        yb, sb, cb, zb, pb = halves[h]
        own_y[h].wait()
        for d in (1, 3, 2):
            landed(yb.at[(y + d) % 4], y_rsem.at[h * 3 + d - 1])
        sb[...] = yb[(theirs >> 1) & 3]
        push(sb, cb.at[c], b_ssem.at[h], b_rsem.at[h], sibling)

        @pl.when(far == 0)
        def _():
            end_copy(h, 1, yb.at[3 * c]).start()
            end_copy(h, 3, yb.at[3 * c]).start()
            pltpu.make_async_copy(yb.at[3 * c], quarter(c, y, h), e_sem.at[h]).start()

        cb[c] = yb[(mine >> 1) & 3]

    def unit(ref, d):
        return ref.at[(zh + 4 - d) % 4]

    def zsem(sem, h, n):
        return sem.at[h * 6 + n]

    def stage_core(h):
        yb, sb, cb, zb, pb = halves[h]
        landed(cb.at[other], b_rsem.at[h])
        zb[...] = cb[mine & 1]
        push(unit(zb, 2), zin[h].at[0], zsem(z_ssem, h, 0), zsem(z_rsem, h, 0), at_z(3))
        push(unit(zb, 3), zin[h].at[1], zsem(z_ssem, h, 1), zsem(z_rsem, h, 1), at_z(1))

    zo = mine >> 3

    def stage_reduce(h):
        yb, sb, cb, zb, pb = halves[h]
        landed(zin[h].at[0], zsem(z_rsem, h, 0))
        zmid[h][...] = jnp.where(zo == (zh + 1) % 4, zin[h][0], zb[(zh + 3) % 4])
        push(zmid[h], zin[h].at[2], zsem(z_ssem, h, 2), zsem(z_rsem, h, 2), at_z(3))

        @pl.when(jnp.logical_or(far == 1, far == 3))
        def _():
            landed(quarter(c, y, h), a_rsem.at[h])

        @pl.when(far == (1 if h == 0 else 3))
        def _():
            end_copy(h, 1 if h == 0 else 3, quarter(c, y, h)).start()

    def stage_root(h):
        yb, sb, cb, zb, pb = halves[h]
        landed(zin[h].at[1], zsem(z_rsem, h, 1))
        landed(zin[h].at[2], zsem(z_rsem, h, 2))
        whole = jnp.where(zo == zh, zb[zh], jnp.where(zo == (zh + 3) % 4, zin[h][1], zin[h][2]))
        pb[zh] = whole
        push(unit(pb, 0), unit(pb, 0), zsem(z_ssem, h, 3), zsem(z_rsem, h, 3), at_z(1))
        push(unit(pb, 0), unit(pb, 0), zsem(z_ssem, h, 4), zsem(z_rsem, h, 4), at_z(3))

    def relay(item, j, h, i, d):
        n = (i * 4 + d) * 2 + h
        push(quarter(item, j, h), quarter(item, j, h), r_ssem.at[n], r_rsem.at[n], sibling)

    def stage_pass(h):
        yb, sb, cb, zb, pb = halves[h]
        landed(unit(pb, 1), zsem(z_rsem, h, 3))
        push(unit(pb, 1), unit(pb, 1), zsem(z_ssem, h, 5), zsem(z_rsem, h, 5), at_z(1))

    def spread_own(h, i, src):
        item = c + 2 * i
        for d in (1, 3):
            push(src, quarter(item, y, h), t_ssem.at[(i * 3 + d - 1) * 2 + h], t_rsem.at[(i * 3 + 3 - d) * 2 + h], at_y(d))
        n = (i * 4) * 2 + h
        push(src, quarter(item, y, h), r_ssem.at[n], r_rsem.at[n], sibling)

    def stage_end(h):
        yb, sb, cb, zb, pb = halves[h]

        @pl.when(far == 2)
        def _():
            landed(quarter(c, y, h), a_rsem.at[h])

        @pl.when(far == 0)
        def _():
            pltpu.make_async_copy(yb.at[3 * c], quarter(c, y, h), e_sem.at[h]).wait()

        spread_own(h, 0, quarter(c, y, h))

    def stage_z(h):
        yb, sb, cb, zb, pb = halves[h]
        landed(unit(pb, 3), zsem(z_rsem, h, 4))
        landed(unit(pb, 2), zsem(z_rsem, h, 5))
        copy_here(pb, quarter(c + 2, y, h))
        spread_own(h, 1, pb)

    def end_drain(h):
        @pl.when(far == 0)
        def _():
            end_copy(h, 1, quarter(c, y, h)).wait_send()
            end_copy(h, 3, quarter(c, y, h)).wait_send()

        @pl.when(far == (1 if h == 0 else 3))
        def _():
            end_copy(h, 1 if h == 0 else 3, quarter(c, y, h)).wait_send()

    def stage_spread(h):
        for i in range(2):
            item = c + 2 * i
            for d in (3, 1):
                j = (y + d) % 4
                landed(quarter(item, j, h), t_rsem.at[(i * 3 + d - 1) * 2 + h])
                if (i == 0 and d == 3) or (i == 1 and d == 1):
                    push(
                        quarter(item, j, h), quarter(item, j, h), t_ssem.at[(i * 3 + 1) * 2 + h], t_rsem.at[(i * 3 + 1) * 2 + h],
                        at_y(1 if i == 0 else 3),
                    )
                relay(item, j, h, i, d)

    def stage_far(h):
        for i in range(2):
            item = c + 2 * i
            j = (y + 2) % 4
            landed(quarter(item, j, h), t_rsem.at[(i * 3 + 1) * 2 + h])
            relay(item, j, h, i, 2)

    def rotary_tables():
        first, stop, _ = slot_tables(len_ref[...], order_ref[...], pref_ref[...])
        tok = (lax.broadcasted_iota(jnp.int32, (1, TOK), 1) + s * TOK).astype(F32)
        start = jnp.max(jnp.where(stop <= tok, jnp.broadcast_to(stop, (REQS, TOK)), 0.0), axis=0, keepdims=True)
        place = tok - start + float(PREFIX)
        angle = freq_ref[...] * place
        cos_buf[...] = jnp.cos(angle)
        sin_buf[...] = jnp.sin(angle)

    def turn_weights(i):
        @pl.loop(i * 9, i * 9 + 9)
        def _(f):
            rows = pl.ds(pl.multiple_of(f * 128, 128), 128)
            g = gain_ref[pl.ds(f, 1), :]
            for cb in range(4):
                w = w_buf[rows, cb * 128:(cb + 1) * 128].astype(F32).T
                wt[cb * 128:(cb + 1) * 128, rows] = (w * g).astype(BF16)

    def multiply(pair, begin):
        rows = pl.multiple_of(pair * 1152, 128)

        @pl.loop(0, 2)
        def _(m):
            mm = pl.ds(pl.multiple_of(m * 256, 256), 256)
            part = jnp.dot(wt[mm, pl.ds(rows, 1152)], h_buf[pl.ds(rows, 1152), :], preferred_element_type=F32)
            acc[mm, :] = part if begin else acc[mm, :] + part

        @pl.loop(0, 9)
        def _(b):
            v = h_buf[pl.ds(pl.multiple_of(rows + b * 128, 128), 128), :].astype(F32)
            v = v * v
            tot = v[0:8]
            for e in range(1, 16):
                tot = tot + v[e * 8:(e + 1) * 8]
            sq[...] = sq[...] + tot

    sq[...] = jnp.zeros_like(sq)
    for cp in weights:
        cp.wait()

    def finish():
        scale = lax.rsqrt(jnp.sum(sq[...], axis=0, keepdims=True) * (1.0 / WIDTH) + EPS)
        cos, sin = cos_buf[...], sin_buf[...]

        def turned(r0):
            a = acc[r0:r0 + 64, :] * scale
            b = acc[r0 + 64:r0 + 128, :] * scale
            return a * cos - b * sin, b * cos + a * sin

        a, b = turned(256)
        kt = jnp.concatenate([a, b], axis=0)
        vt = (acc[384:512, :] * scale).astype(BF16)
        for blk in range(4):
            kv_own[blk, 0:128, :] = kt[:, blk * 128:(blk + 1) * 128].T.astype(BF16)
            kv_own[blk, 128:256, :] = vt[:, blk * 128:(blk + 1) * 128]

    def queries():
        scale = lax.rsqrt(jnp.sum(sq[...], axis=0, keepdims=True) * (1.0 / WIDTH) + EPS)
        cos, sin = cos_buf[...], sin_buf[...]

        def turned(r0):
            a = acc[r0:r0 + 64, :] * scale
            b = acc[r0 + 64:r0 + 128, :] * scale
            return a * cos - b * sin, b * cos + a * sin

        for hd in range(2):
            a, b = turned(hd * 128)
            q_out[hd * 128:hd * 128 + 64, :] = a.astype(BF16)
            q_out[hd * 128 + 64:hd * 128 + 128, :] = b.astype(BF16)

    def kv(slot, g):
        return kv_out.at[pl.ds(slot * 4 + g * 2, 2)]

    sib_slot = (4 * other, 4 - 2 * other, 2 - 2 * other)
    my_slot = (4 * c, 4 - 2 * c, 2 - 2 * c)

    def kv_way(n, g, src, dst, where):
        return remote(src, dst, k_ssem.at[n * 2 + g], k_rsem.at[n * 2 + g], where)

    def transit(g):
        return kv_via.at[pl.ds(g * 2, 2)]

    def kv_start():
        for g in range(2):
            src = kv_own.at[pl.ds(g * 2, 2)]

            @pl.when(y >= 2)
            def _():
                kv_way(5, g, src, transit(g), at_z(1)).start()

            @pl.when(y <= 2)
            def _():
                kv_way(0, g, src, kv(3, g), at_y(1)).start()

        for g in range(2):
            src = kv_own.at[pl.ds(g * 2, 2)]
            kv_way(2, g, src, kv(sib_slot[0], g), sibling).start()
        copy_here(kv_own, kv_out.at[pl.ds(20, 4)])

    def kv_transit(g):
        @pl.when(y == 3)
        def _():
            landed(transit(g), k_rsem.at[10 + g])
            kv_way(0, g, transit(g), kv(3, g), at_y(1)).start()

        @pl.when(y == 2)
        def _():
            landed(transit(g), k_rsem.at[10 + g])
            kv_way(6, g, transit(g), kv(1, g), at_y(2)).start()

    def kv_first(g):
        landed(kv(3, g), k_rsem.at[g])

        @pl.when(y <= 2)
        def _():
            kv_way(1, g, kv(3, g), kv(1, g), at_y(1)).start()

        kv_way(3, g, kv(3, g), kv(sib_slot[1], g), sibling).start()

    def kv_second(g):
        @pl.when(y >= 1)
        def _():
            landed(kv(1, g), k_rsem.at[2 + g])

        @pl.when(y == 0)
        def _():
            landed(kv(1, g), k_rsem.at[12 + g])

        kv_way(4, g, kv(1, g), kv(sib_slot[2], g), sibling).start()

    def kv_drain(g):
        own = kv_own.at[pl.ds(g * 2, 2)]
        kv_way(0, g, own, kv(3, g), sibling).wait_send()
        for n in (2, 3, 4):
            kv_way(n, g, own, kv(3, g), sibling).wait_send()

        @pl.when(y <= 2)
        def _():
            kv_way(1, g, own, kv(3, g), sibling).wait_send()

        @pl.when(y >= 2)
        def _():
            kv_way(5, g, own, kv(3, g), sibling).wait_send()

        @pl.when(y == 2)
        def _():
            kv_way(6, g, own, kv(3, g), sibling).wait_send()

    steps = {
        "W": turn_weights, "g1": gather.first, "g2": gather.second, "g3": gather.third, "sy": stage_y, "sc": stage_core,
        "sr": stage_reduce, "so": stage_root, "ss": stage_pass, "se": stage_end,
        "sz": stage_z, "sp": stage_spread, "sf": stage_far, "kt": kv_transit, "k1": kv_first, "k2": kv_second,
        "rot": lambda _: rotary_tables(), "kv": lambda _: kv_start(), "fin": lambda _: finish(), "q": lambda _: queries(),
        "M": lambda i: multiply(
            (l * 2 + x // 2, l * 2 + 1 - x // 2, (1 - l) * 2 + x // 2, (1 - l) * 2 + 1 - x // 2)[i], i == 0
        ),
    }
    groups = {"W": "mm", "M": "mm", "rot": "mm", "fin": "mm", "q": "mm", "g1": "gather", "g2": "gather", "g3": "gather",
              "kv": "kv", "kt": "kv", "k1": "kv", "k2": "kv"}
    for name, arg in SCHED:
        if groups.get(name, "prefix") in ON:
            steps[name](arg)
    if "prefix" in ON:
        for i in range(2):
            item = other + 2 * i
            for d in range(4):
                for h in range(2):
                    landed(quarter(item, (y + d) % 4, h), r_rsem.at[(i * 4 + d) * 2 + h])
    if "kv" in ON:
        for n in range(3):
            for g in range(2):
                landed(kv(my_slot[n], g), k_rsem.at[4 + 2 * n + g])
    gather.drain()
    for cp in pending:
        cp.wait_send()
    if "kv" in ON:
        for g in range(2):
            kv_drain(g)
    if "prefix" in ON:
        for h in range(2):
            end_drain(h)
    for cp in local[4 + (2 if "prefix" in ON else 0):]:
        cp.wait()


def kernel_attend(
    owner_s, len_s, order_s, pref_s, len_ref, order_ref, pref_ref, q_ref, kv_ref, f_ref, out_ref, acc, meta, work, item_of
):
    base = lax.axis_index("seq") * TOK
    seen = jnp.int32(0)
    for p in range(4):
        o = owner_s[p]
        inner = jnp.logical_and(o != 0, o != 31)
        item_of[p] = jnp.where(o == 0, 0, jnp.where(o == 31, 1, 2 + jnp.minimum(seen, 1)))
        seen = seen + inner.astype(jnp.int32)

    def look(r, carry):
        at = carry[0]
        req = order_s[r]
        stop = at + len_s[req]
        bit = jnp.int32(1) << pref_s[req]
        out = [stop]
        for rb in range(4):
            lo = base + rb * 128
            hit = jnp.logical_and(at < lo + 128, stop > lo)
            out.append(jnp.where(hit, carry[1 + 2 * rb] | bit, carry[1 + 2 * rb]))
            out.append(jnp.where(jnp.logical_and(at <= lo, stop > lo), at, carry[2 + 2 * rb]))
        return tuple(out)

    zero = jnp.int32(0)
    found = lax.fori_loop(0, REQS, look, (zero,) * 9)
    count = jnp.int32(0)
    for rb in range(4):
        for p in range(4):
            work[count] = rb * 4 + p
            count = count + ((found[1 + 2 * rb] >> p) & 1)

    first, stop, prefix = slot_tables(len_ref[...], order_ref[...], pref_ref[...])
    for rb in range(4):
        tok = (lax.broadcasted_iota(jnp.int32, (1, 256), 1) % 128 + (base + rb * 128)).astype(F32)
        begin = jnp.max(jnp.where(stop <= tok, jnp.broadcast_to(stop, (REQS, 256)), 0.0), axis=0, keepdims=True)
        inside = jnp.logical_and(first <= tok, tok < stop)
        pref = jnp.sum(jnp.where(inside, jnp.broadcast_to(prefix, (REQS, 256)), 0.0), axis=0, keepdims=True)
        meta[rb, 0:1, :] = tok
        meta[rb, 1:2, :] = begin
        meta[rb, 2:3, :] = pref
    c1 = float(QSCALE ** -0.5 / SOFTCAP)
    c2 = float(SOFTCAP * math.log2(math.e))
    ones = jnp.ones((16, KEYS), BF16)

    def queries(rb):
        lanes = pl.ds(pl.multiple_of(rb * 128, 128), 128)
        return jnp.concatenate([q_ref[0:128, lanes], q_ref[128:256, lanes]], axis=1)

    def weigh(k2, qt):
        sc = jnp.dot(k2, qt, preferred_element_type=F32)
        return jnp.exp2(jnp.tanh(sc * c1) * c2)

    for rb in range(4):
        qt = queries(rb)
        tok = meta[rb, 0:1, :]
        begin = meta[rb, 1:2, :]
        acc[rb] = jnp.zeros((144, 256), F32)
        chunks = (base + (rb + 1) * 128 - found[2 + 2 * rb] + KEYS - 1) // KEYS

        @pl.loop(0, chunks)
        def _(n):
            u = 20 + rb + 1 - (n + 1) * (KEYS // 128)
            k2 = jnp.concatenate([kv_ref[u + e, 0:128, :] for e in range(KEYS // 128)], axis=0)
            v2 = jnp.concatenate([kv_ref[u + e, 128:256, :] for e in range(KEYS // 128)], axis=1)
            key = (lax.broadcasted_iota(jnp.int32, (KEYS, 1), 0) + (base - 2560 + u * 128)).astype(F32)
            ok = jnp.logical_and(key <= tok, key >= begin)
            w = jnp.where(ok, weigh(k2, qt), 0.0).astype(BF16)
            acc[rb] += jnp.dot(jnp.concatenate([v2, ones], axis=0), w, preferred_element_type=F32)

    @pl.loop(0, count)
    def _(i):
        code = work[i]
        rb, p = code >> 2, code & 3
        item = item_of[p]
        qt = queries(rb)
        ws = []
        vs = []
        for n in range(PREFIX // KEYS):
            u = n * (KEYS // 64)
            k2 = jnp.concatenate([f_ref[item, u + 2 * e] for e in range(KEYS // 128)], axis=0)
            vs += [f_ref[item, u + 2 * e + 1] for e in range(KEYS // 128)]
            ws.append(weigh(k2, qt).astype(BF16))
        v2 = jnp.concatenate([jnp.concatenate(vs, axis=1), jnp.ones((16, PREFIX), BF16)], axis=0)
        part = jnp.dot(v2, jnp.concatenate(ws, axis=0), preferred_element_type=F32)
        acc[rb] += jnp.where(meta[rb, 2:3, :] == p.astype(F32), part, 0.0)

    for rb in range(4):
        lanes = slice(rb * 128, rb * 128 + 128)
        att = acc[rb, 0:128, :] / acc[rb, 128:129, :]
        out_ref[0:128, lanes] = att[:, 0:128].astype(BF16)
        out_ref[128:256, lanes] = att[:, 128:256].astype(BF16)


def kernel_out(
    att_ref, wo_hbm, h_ref, gain_ref, out_ref, g_buf, wo_buf, acc, gcol, sums, g_ssem, g_rsem, q_ssem, q_rsem, local_sem
):
    s = lax.axis_index("seq")
    t = lax.axis_index("tp")
    l, x = t // 4, t % 4
    gather = Gather(OUT_PIECES, att_ref, g_buf, g_ssem, g_rsem, 256, x, l)

    def peer(d):
        return {"tp": (t + d) % 8}

    barrier = pltpu.get_barrier_semaphore()
    for d in range(1, 8):
        pl.semaphore_signal(barrier, inc=1, device_id=peer(d), device_id_type=MESH)
    wo_copy = pltpu.make_async_copy(wo_hbm, wo_buf, local_sem.at[0])
    own_copy = pltpu.make_async_copy(att_ref, g_buf.at[pl.ds(pl.multiple_of(t * 256, 256), 256)], local_sem.at[1])
    wo_copy.start()
    own_copy.start()
    pl.semaphore_wait(barrier, 7)
    gather.start()

    g5 = gain_ref[t]
    for b in range(5):
        gcol[b * 128:(b + 1) * 128, :] = jnp.broadcast_to(g5[b:b + 1, :], (128, 128)).T
    wo_copy.wait()
    own_copy.wait()

    def multiply(dx, dl, begin):
        shard = ((l + dl) % 2) * 4 + (x + dx) % 4
        rows = pl.ds(pl.multiple_of(shard * 256, 256), 256)

        @pl.loop(0, 4)
        def _(m):
            mm = pl.ds(pl.multiple_of(m * 144, 16), 144)
            part = jnp.dot(wo_buf[mm, rows], g_buf[rows, :], preferred_element_type=F32)
            acc[mm, :] = part if begin else acc[mm, :] + part

    multiply(0, 0, True)
    for k in range(4):
        gather.first(k)
    multiply(1, 0, False)
    multiply(3, 0, False)
    multiply(0, 1, False)
    for k in range(4):
        gather.second(k)
    multiply(2, 0, False)
    multiply(1, 1, False)
    multiply(3, 1, False)
    for k in range(4):
        gather.third(k)
    multiply(2, 1, False)

    tot = jnp.zeros((8, TOK), F32)
    for b in range(72):
        v = acc[b * 8:(b + 1) * 8, :]
        tot = tot + v * v
    sums[t] = tot
    copies = []
    for d in range(1, 8):
        cp = remote(sums.at[t], sums.at[t], q_ssem.at[d - 1], q_rsem.at[7 - d], peer(d))
        cp.start()
        copies.append(cp)
    for d in range(1, 8):
        here = sums.at[(t + d) % 8]
        remote(here, here, q_ssem.at[0], q_rsem.at[d - 1], peer(1)).wait_recv()
    tot = sums[0]
    for d in range(1, 8):
        tot = tot + sums[d]
    scale = lax.rsqrt(jnp.sum(tot, axis=0, keepdims=True) * (1.0 / WIDTH) + EPS)
    for b in range(9):
        rows = slice(b * 64, b * 64 + 64)
        g = gcol[rows, :]
        for n in range(4):
            cols = slice(n * 128, n * 128 + 128)
            post = acc[rows, cols] * scale[:, cols] * g
            out_ref[rows, cols] = (h_ref[rows, cols].astype(F32) + post).astype(BF16)
    gather.drain()
    for cp in copies:
        cp.wait_send()


def on_device(
    hidden_in, pre_gain, post_gain, w_query, key_weight, value_weight, w_out, cache, suffix_len, request_order,
    request_prefix, prefix_owner,
):
    hbm = pl.BlockSpec(memory_space=pltpu.MemorySpace.HBM)
    vmem = pl.BlockSpec(memory_space=pltpu.VMEM)
    smem = pl.BlockSpec(memory_space=pltpu.SMEM)
    dma = pltpu.SemaphoreType.DMA
    h_t = hidden_in.T
    len_row = suffix_len.reshape(1, REQS)
    order_row = request_order.reshape(1, REQS)
    pref_row = request_prefix.reshape(1, REQS)
    freq = jnp.asarray((10000.0 ** (-2.0 * np.arange(64) / HEAD)).astype(np.float32).reshape(64, 1))
    n = len(IN_PIECES)
    sends = 7 * n
    one = pltpu.VMEM((128, 128), BF16)
    three = pltpu.VMEM((3, 128, 128), BF16)
    half = pltpu.VMEM((4, 128, 128), BF16)
    four = pltpu.VMEM((4, 4, 128, 128), BF16)
    two = pltpu.VMEM((2, 4, 128, 128), BF16)
    q, kv, spread = pl.pallas_call(
        kernel_in,
        out_shape=(
            jax.ShapeDtypeStruct((256, TOK), BF16),
            jax.ShapeDtypeStruct((24, 256, 128), BF16),
            jax.ShapeDtypeStruct((4, 32, 128, 128), BF16),
        ),
        in_specs=[smem, vmem, vmem, vmem, vmem, vmem, hbm, hbm, hbm, hbm, vmem],
        out_specs=(vmem, vmem, vmem),
        scratch_shapes=[
            pltpu.VMEM((WIDTH, TOK), BF16),
            pltpu.VMEM((WIDTH, 512), BF16),
            pltpu.VMEM((512, WIDTH), BF16),
            pltpu.VMEM((512, TOK), F32),
            pltpu.VMEM((8, TOK), F32),
            pltpu.VMEM((64, TOK), F32),
            pltpu.VMEM((64, TOK), F32),
            pltpu.VMEM((32, 128, 128), BF16),
            four, four, half, half, two, two, half, half, half, half, three, three, one, one,
            pltpu.VMEM((4, 256, 128), BF16), pltpu.VMEM((4, 256, 128), BF16),
            dma((sends,)), dma((8 * n,)), dma((6,)), dma((6,)), dma((2,)), dma((2,)), dma((12,)), dma((12,)),
            dma((12,)), dma((12,)), dma((4,)), dma((2,)), dma((2,)), dma((16,)), dma((16,)), dma((14,)), dma((14,)), dma((12,)),
        ],
        compiler_params=pltpu.CompilerParams(collective_id=0, has_side_effects=True, vmem_limit_bytes=34 << 20),
    )(
        prefix_owner, len_row, order_row, pref_row, pre_gain.reshape(36, 128), freq,
        h_t, w_query, key_weight, value_weight, cache.reshape(4096, 128),
    )
    att = pl.pallas_call(
        kernel_attend,
        out_shape=jax.ShapeDtypeStruct((256, TOK), BF16),
        in_specs=[smem] * 4 + [vmem] * 6,
        out_specs=vmem,
        scratch_shapes=[
            pltpu.VMEM((4, 144, 256), F32),
            pltpu.VMEM((4, 8, 256), F32),
            pltpu.SMEM((17,), jnp.int32),
            pltpu.SMEM((4,), jnp.int32),
        ],
        compiler_params=pltpu.CompilerParams(vmem_limit_bytes=16 << 20),
    )(prefix_owner, suffix_len, request_order, request_prefix, len_row, order_row, pref_row, q, kv, spread)
    gains = jnp.pad(post_gain.reshape(8, SHARD), ((0, 0), (0, 64))).reshape(8, 5, 128)
    out = pl.pallas_call(
        kernel_out,
        out_shape=jax.ShapeDtypeStruct((SHARD, TOK), BF16),
        in_specs=[vmem, hbm, vmem, vmem],
        out_specs=vmem,
        scratch_shapes=[
            pltpu.VMEM((2048, TOK), BF16),
            pltpu.VMEM((SHARD, 2048), BF16),
            pltpu.VMEM((SHARD, TOK), F32),
            pltpu.VMEM((640, 128), F32),
            pltpu.VMEM((8, 8, TOK), F32),
            dma((7 * len(OUT_PIECES),)), dma((8 * len(OUT_PIECES),)), dma((7,)), dma((7,)), dma((2,)),
        ],
        compiler_params=pltpu.CompilerParams(collective_id=1, has_side_effects=True, vmem_limit_bytes=16 << 20),
    )(att, w_out.T, h_t, gains)
    return out.T


def solution(mesh):
    placed = (
        P("seq", "tp"), P(), P(), P(None, "tp"), P(None, "tp"), P(None, "tp"), P(None, "tp"), P("seq", None, "tp"),
        P(), P(), P(), P(),
    )
    return jax.shard_map(on_device, mesh=mesh, in_specs=placed, out_specs=P("seq", "tp"), check_vma=False)
```

```python
import math

import jax
import jax.numpy as jnp
import numpy as np
from jax import lax
from jax.experimental import pallas as pl
from jax.experimental.pallas import tpu as pltpu
from jax.sharding import PartitionSpec as P

MESH = pl.DeviceIdType.MESH
WIDTH = 4608
HEAD = 128
QSCALE = 144
PREFIX = 2048
TOK = 512
REQS = 48
SHARD = 576
IN_PIECES = (("P", "R"), ("P", "L"), ("P", "R"), ("P", "L"))
OUT_PIECES = (("P", "R"), ("P", "L"), ("Q", "R"), ("Q", "L"))
SOFTCAP = 50.0
EPS = 1e-6
KEYS = 512
ON = ("mm", "gather", "prefix", "kv")
SCHED = (
    ("W", 0), ("g1", 0), ("g1", 1), ("gs", 0), ("sy", 0), ("sc", 0), ("W", 1), ("sy", 1), ("g2", 0),
    ("sc", 1), ("W", 2), ("er", 0), ("sy", 2), ("sr", 0), ("g2", 1), ("sc", 2), ("W", 3), ("er", 1),
    ("sy", 3), ("sr", 1), ("g1", 2), ("sc", 3), ("M", 0), ("er", 2), ("se", 0), ("sz", 0), ("sr", 2),
    ("g1", 3), ("rot", 0), ("er", 3), ("se", 1), ("sz", 1), ("sr", 3), ("M", 1), ("M", 2), ("g3", 0),
    ("g3", 1), ("sp", 0), ("se", 2), ("sz", 2), ("M", 3), ("fin", 0), ("kv", 0), ("q", 0), ("se", 3),
    ("sz", 3), ("sp", 1), ("sf", 0), ("g2", 2), ("M", 4), ("g2", 3), ("sp", 2), ("sf", 1), ("kt", 0),
    ("M", 5), ("M", 6), ("sp", 3), ("sf", 2), ("k1", 0), ("sf", 3), ("g3", 2), ("k2", 0), ("g3", 3),
    ("M", 7), ("fin", 1), ("kv", 1), ("q", 1), ("kt", 1), ("k1", 1), ("k2", 1),
)
F32 = jnp.float32
BF16 = jnp.bfloat16


def remote(src, dst, ssem, rsem, where):
    return pltpu.make_async_remote_copy(
        src_ref=src, dst_ref=dst, send_sem=ssem, recv_sem=rsem, device_id=where, device_id_type=MESH
    )


class Gather:
    def __init__(self, pieces, halves, own, buf, ssem, rsem, rows, x, l):
        self.pieces = pieces
        self.own, self.buf, self.ssem, self.rsem, self.rows = own, buf, ssem, rsem, rows
        self.x, self.l = x, l
        self.count = 0
        self.started = []
        self.n = len(pieces)
        self.prow = rows // 2 if halves else rows // self.n
        self.halves = halves

    def target(self, way):
        x, l = self.x, self.l
        if way == "R":
            return {"tp": l * 4 + (x + 1) % 4}
        if way == "L":
            return {"tp": l * 4 + (x + 3) % 4}
        return {"tp": (1 - l) * 4 + x}

    def place(self, dx, dl, k):
        shard = ((self.l + dl) % 2) * 4 + (self.x + dx) % 4
        return self.part(self.buf, shard * self.rows, k)

    def part(self, ref, base, k):
        if not self.halves:
            return ref.at[pl.ds(pl.multiple_of(base + k * self.prow, 16), self.prow)]
        rows = pl.ds(pl.multiple_of(base + (k % 2) * self.prow, 16), self.prow)
        return ref.at[rows, pl.ds((k // 2) * (TOK // 2), TOK // 2)]

    def send(self, dx, dl, k, way):
        src = self.place(dx, dl, k)
        if dx == 0 and dl == 0:
            src = self.part(self.own, 0, k)
        rdx, rdl = dx, dl
        if way == "R":
            rdx = (dx + 3) % 4
        elif way == "L":
            rdx = (dx + 1) % 4
        else:
            rdl = 1 - dl
        copy = remote(
            src, self.place(dx, dl, k), self.ssem.at[self.count], self.rsem.at[(rdl * 4 + rdx) * self.n + k], self.target(way)
        )
        copy.start()
        self.count += 1
        self.started.append(copy)

    def wait(self, dx, dl, k):
        here = self.place(dx, dl, k)
        remote(here, here, self.ssem.at[0], self.rsem.at[(dl * 4 + dx) * self.n + k], self.target("R")).wait_recv()

    def start(self, k0, k1):
        for k in range(k0, k1):
            for way in ("R", "L", "Z"):
                self.send(0, 0, k, way)

    def first(self, k):
        kind, way = self.pieces[k]
        self.wait(3, 0, k)
        if way == "R":
            self.send(3, 0, k, "R")
        if kind == "Q":
            self.send(3, 0, k, "Z")
        self.wait(1, 0, k)
        if way == "L":
            self.send(1, 0, k, "L")
        if kind == "Q":
            self.send(1, 0, k, "Z")
        self.wait(0, 1, k)
        if kind == "P":
            self.send(0, 1, k, "R")
            self.send(0, 1, k, "L")

    def second(self, k):
        kind, way = self.pieces[k]
        self.wait(2, 0, k)
        if kind == "Q":
            self.send(2, 0, k, "Z")
        self.wait(3, 1, k)
        if kind == "P" and way == "R":
            self.send(3, 1, k, "R")
        self.wait(1, 1, k)
        if kind == "P" and way == "L":
            self.send(1, 1, k, "L")

    def third(self, k):
        self.wait(2, 1, k)

    def drain(self):
        for copy in self.started:
            copy.wait_send()


def slot_tables(len_row, order_row, prefix_row):
    len_row, order_row, prefix_row = (v.astype(F32) for v in (len_row, order_row, prefix_row))
    a = lax.broadcasted_iota(jnp.int32, (REQS, REQS), 0)
    b = lax.broadcasted_iota(jnp.int32, (REQS, REQS), 1)
    order_col = jnp.sum(jnp.where(a == b, jnp.broadcast_to(order_row, (REQS, REQS)), 0.0), axis=1, keepdims=True)
    chosen = order_col == b.astype(F32)
    length = jnp.sum(jnp.where(chosen, jnp.broadcast_to(len_row, (REQS, REQS)), 0.0), axis=1, keepdims=True)
    prefix = jnp.sum(jnp.where(chosen, jnp.broadcast_to(prefix_row, (REQS, REQS)), 0.0), axis=1, keepdims=True)
    length_row = jnp.sum(jnp.where(a == b, jnp.broadcast_to(length, (REQS, REQS)), 0.0), axis=0, keepdims=True)
    stop = jnp.sum(jnp.where(b <= a, jnp.broadcast_to(length_row, (REQS, REQS)), 0.0), axis=1, keepdims=True)
    return stop - length, stop, prefix


def kernel_in(*refs):
    (
        owner_ref, len_ref, order_ref, pref_ref, gain_ref, freq_ref, h_hbm, wq_hbm, wk_hbm, wv_hbm, cache_hbm,
        q_out, kv_out, f_out, h_buf, w_buf, wt, acc, sq, cos_buf, sin_buf, cache_buf, cache_f,
    ) = refs[:23]
    parts = refs[23:47]
    (
        kv_own, kv_via, g_ssem, g_rsem, y_ssem, y_rsem, b_ssem, b_rsem, z_ssem, z_rsem, t_ssem, t_rsem,
        a_ssem, a_rsem, e_sem, r_ssem, r_rsem, k_ssem, k_rsem, local_sem,
    ) = refs[47:]
    s = lax.axis_index("seq")
    t = lax.axis_index("tp")
    zh, y, c = s // 8, (s // 2) % 4, s % 2
    l, x = t // 4, t % 4
    other = 1 - c
    sibling = {"seq": zh * 8 + y * 2 + other}

    def at_y(d):
        return {"seq": zh * 8 + ((y + d) % 4) * 2 + c}

    def at_z(d):
        return {"seq": ((zh + d) % 4) * 8 + y * 2 + c}

    gather = Gather(IN_PIECES, True, h_hbm, h_buf, g_ssem, g_rsem, SHARD, x, l)

    barrier = pltpu.get_barrier_semaphore()
    peers = [gather.target("R"), gather.target("L"), gather.target("Z"), sibling]
    peers += [at_y(1), at_y(2), at_y(3), at_z(1), at_z(2), at_z(3)]
    for peer in peers:
        pl.semaphore_signal(barrier, inc=1, device_id=peer, device_id_type=MESH)

    local = []

    def copy_here(src, dst):
        cp = pltpu.make_async_copy(src, dst, local_sem.at[len(local)])
        cp.start()
        local.append(cp)
        return cp

    cache_copy = copy_here(cache_hbm, cache_buf)
    weights = [
        copy_here(wq_hbm, w_buf.at[:, pl.ds(0, 256)]),
        copy_here(wk_hbm, w_buf.at[:, pl.ds(256, 128)]),
        copy_here(wv_hbm, w_buf.at[:, pl.ds(384, 128)]),
        copy_here(h_hbm, h_buf.at[pl.ds(pl.multiple_of(t * SHARD, 16), SHARD)]),
    ]
    pl.semaphore_wait(barrier, len(peers))
    if "gather" in ON:
        gather.start(0, 2)

    to = lax.broadcasted_iota(jnp.int32, (256, 256), 0)
    of = lax.broadcasted_iota(jnp.int32, (256, 256), 1)
    apart = jnp.where(of == 2 * to - jnp.where(to < 128, 0, 255), 1.0, 0.0).astype(BF16)

    def split_cache(h):
        for j in range(4):
            b = j * 4 + h
            both = jnp.dot(apart, cache_buf[b * 256:(b + 1) * 256, :], preferred_element_type=F32)
            values = both[128:256].T.astype(BF16)
            for e in range(2):
                cache_f[b * 4 + e] = both[e * 64:e * 64 + 64].astype(BF16)
                cache_f[b * 4 + 2 + e] = values[e * 64:e * 64 + 64]

    cache_copy.wait()

    halves = [parts[h * 6:h * 6 + 5] for h in range(4)]
    zin = [parts[h * 6 + 5] for h in range(4)]
    pending = []

    def push(src, dst, ssem, rsem, where):
        cp = remote(src, dst, ssem, rsem, where)
        cp.start()
        pending.append(cp)

    def landed(ref, rsem):
        remote(ref, ref, y_ssem.at[0], rsem, sibling).wait_recv()

    own_y = []
    for h in (range(4) if "prefix" in ON else ()):
        yb = halves[h][0]
        split_cache(h)
        for d in (1, 3, 2):
            j = (y + d) % 4
            push(cache_f.at[pl.ds(j * 16 + h * 4, 4)], yb.at[y], y_ssem.at[h * 3 + d - 1], y_rsem.at[h * 3 + 3 - d], at_y(d))
        own_y.append(copy_here(cache_f.at[pl.ds(y * 16 + h * 4, 4)], yb.at[y]))

    oc = jnp.int32(-1)
    od = jnp.int32(-1)
    for p in range(4):
        o = owner_ref[p]
        inner = jnp.logical_and(o != 0, o != 31)
        fresh = oc < 0
        od = jnp.where(jnp.logical_and(inner, jnp.logical_not(fresh)), o, od)
        oc = jnp.where(jnp.logical_and(inner, fresh), o, oc)
    oc = jnp.clip(oc, 0, 31)
    od = jnp.clip(od, 0, 31)
    mine = jnp.where(c == 0, oc, od)
    theirs = jnp.where(c == 0, od, oc)

    def quarter(item, j, h):
        return f_out.at[item, pl.ds(j * 16 + h * 4, 4)]

    far = (zh - 3 * c) % 4

    def end_copy(h, d, src):
        return remote(src, quarter(c, y, h), a_ssem.at[h * 2 + d // 2], a_rsem.at[h], at_z(d))

    def stage_y(h):
        yb, sb, cb, zb, pb = halves[h]
        own_y[h].wait()
        for d in (1, 3, 2):
            landed(yb.at[(y + d) % 4], y_rsem.at[h * 3 + d - 1])
        sb[...] = yb[(theirs >> 1) & 3]
        push(sb, cb.at[c], b_ssem.at[h], b_rsem.at[h], sibling)

        @pl.when(far == 0)
        def _():
            end_copy(h, 1, yb.at[3 * c]).start()
            end_copy(h, 3, yb.at[3 * c]).start()
            pltpu.make_async_copy(yb.at[3 * c], quarter(c, y, h), e_sem.at[h]).start()

        cb[c] = yb[(mine >> 1) & 3]

    def unit(ref, d):
        return ref.at[(zh + 4 - d) % 4]

    def zsem(sem, h, n):
        return sem.at[h * 6 + n]

    def stage_core(h):
        yb, sb, cb, zb, pb = halves[h]
        landed(cb.at[other], b_rsem.at[h])
        zb[...] = cb[mine & 1]
        for d in (1, 3, 2):
            push(unit(zb, d), zin[h].at[d - 1], zsem(z_ssem, h, d - 1), zsem(z_rsem, h, d - 1), at_z(4 - d))

    zo = mine >> 3

    def stage_reduce(h):
        yb, sb, cb, zb, pb = halves[h]
        whole = zb[zh]
        for d in (1, 3, 2):
            landed(zin[h].at[d - 1], zsem(z_rsem, h, d - 1))
            whole = jnp.where(zo == (zh + d) % 4, zin[h][d - 1], whole)
        pb[zh] = whole
        for d in (1, 3, 2):
            push(unit(pb, 0), unit(pb, 0), zsem(z_ssem, h, 2 + d), zsem(z_rsem, h, 2 + d), at_z(d))

    def stage_relay(h):
        @pl.when(jnp.logical_or(far == 1, far == 3))
        def _():
            landed(quarter(c, y, h), a_rsem.at[h])

        @pl.when(far == (1 if h % 2 == 0 else 3))
        def _():
            end_copy(h, 1 if h % 2 == 0 else 3, quarter(c, y, h)).start()

    def relay(item, j, h, i, d):
        n = (i * 4 + d) * 4 + h
        push(quarter(item, j, h), quarter(item, j, h), r_ssem.at[n], r_rsem.at[n], sibling)

    def spread_own(h, i, src):
        item = c + 2 * i
        for d in (1, 3):
            push(src, quarter(item, y, h), t_ssem.at[(i * 3 + d - 1) * 4 + h], t_rsem.at[(i * 3 + 3 - d) * 4 + h], at_y(d))
        n = (i * 4) * 4 + h
        push(src, quarter(item, y, h), r_ssem.at[n], r_rsem.at[n], sibling)

    def stage_end(h):
        yb, sb, cb, zb, pb = halves[h]

        @pl.when(far == 2)
        def _():
            landed(quarter(c, y, h), a_rsem.at[h])

        @pl.when(far == 0)
        def _():
            pltpu.make_async_copy(yb.at[3 * c], quarter(c, y, h), e_sem.at[h]).wait()

        spread_own(h, 0, quarter(c, y, h))

    def stage_z(h):
        yb, sb, cb, zb, pb = halves[h]
        for d in (1, 3, 2):
            landed(unit(pb, d), zsem(z_rsem, h, 2 + d))
        copy_here(pb, quarter(c + 2, y, h))
        spread_own(h, 1, pb)

    def end_drain(h):
        @pl.when(far == 0)
        def _():
            end_copy(h, 1, quarter(c, y, h)).wait_send()
            end_copy(h, 3, quarter(c, y, h)).wait_send()

        @pl.when(far == (1 if h % 2 == 0 else 3))
        def _():
            end_copy(h, 1 if h % 2 == 0 else 3, quarter(c, y, h)).wait_send()

    def stage_spread(h):
        for i in range(2):
            item = c + 2 * i
            for d in (3, 1):
                j = (y + d) % 4
                landed(quarter(item, j, h), t_rsem.at[(i * 3 + d - 1) * 4 + h])
                if (i == 0 and d == 3) or (i == 1 and d == 1):
                    push(
                        quarter(item, j, h), quarter(item, j, h), t_ssem.at[(i * 3 + 1) * 4 + h], t_rsem.at[(i * 3 + 1) * 4 + h],
                        at_y(1 if i == 0 else 3),
                    )
                relay(item, j, h, i, d)

    def stage_far(h):
        for i in range(2):
            item = c + 2 * i
            j = (y + 2) % 4
            landed(quarter(item, j, h), t_rsem.at[(i * 3 + 1) * 4 + h])
            relay(item, j, h, i, 2)

    def rotary_tables():
        first, stop, _ = slot_tables(len_ref[...], order_ref[...], pref_ref[...])
        tok = (lax.broadcasted_iota(jnp.int32, (1, TOK), 1) + s * TOK).astype(F32)
        start = jnp.max(jnp.where(stop <= tok, jnp.broadcast_to(stop, (REQS, TOK)), 0.0), axis=0, keepdims=True)
        place = tok - start + float(PREFIX)
        angle = freq_ref[...] * place
        cos_buf[...] = jnp.cos(angle)
        sin_buf[...] = jnp.sin(angle)

    def turn_weights(i):
        @pl.loop(i * 9, i * 9 + 9)
        def _(f):
            rows = pl.ds(pl.multiple_of(f * 128, 128), 128)
            g = gain_ref[pl.ds(f, 1), :]
            for cb in range(4):
                w = w_buf[rows, cb * 128:(cb + 1) * 128].astype(F32).T
                wt[cb * 128:(cb + 1) * 128, rows] = (w * g).astype(BF16)

    def multiply(pair, g, begin):
        rows = pl.multiple_of(pair * 1152, 128)
        lanes = slice(g * 256, g * 256 + 256)
        for m in range(2):
            mm = slice(m * 256, m * 256 + 256)
            part = jnp.dot(wt[mm, pl.ds(rows, 1152)], h_buf[pl.ds(rows, 1152), lanes], preferred_element_type=F32)
            acc[mm, lanes] = part if begin else acc[mm, lanes] + part

        @pl.loop(0, 9)
        def _(b):
            v = h_buf[pl.ds(pl.multiple_of(rows + b * 128, 128), 128), lanes].astype(F32)
            v = v * v
            tot = v[0:8]
            for e in range(1, 16):
                tot = tot + v[e * 8:(e + 1) * 8]
            sq[:, lanes] = sq[:, lanes] + tot

    sq[...] = jnp.zeros_like(sq)
    for cp in weights:
        cp.wait()

    def turned(r0, g):
        lanes = slice(g * 256, g * 256 + 256)
        scale = lax.rsqrt(jnp.sum(sq[:, lanes], axis=0, keepdims=True) * (1.0 / WIDTH) + EPS)
        cos, sin = cos_buf[:, lanes], sin_buf[:, lanes]
        a = acc[r0:r0 + 64, lanes] * scale
        b = acc[r0 + 64:r0 + 128, lanes] * scale
        return a * cos - b * sin, b * cos + a * sin, scale

    def finish(g):
        a, b, scale = turned(256, g)
        kt = jnp.concatenate([a, b], axis=0)
        vt = (acc[384:512, g * 256:g * 256 + 256] * scale).astype(BF16)
        for e in range(2):
            kv_own[g * 2 + e, 0:128, :] = kt[:, e * 128:(e + 1) * 128].T.astype(BF16)
            kv_own[g * 2 + e, 128:256, :] = vt[:, e * 128:(e + 1) * 128]

    def queries(g):
        lanes = slice(g * 256, g * 256 + 256)
        for hd in range(2):
            a, b, _ = turned(hd * 128, g)
            q_out[hd * 128:hd * 128 + 64, lanes] = a.astype(BF16)
            q_out[hd * 128 + 64:hd * 128 + 128, lanes] = b.astype(BF16)

    def kv(slot, g):
        return kv_out.at[pl.ds(slot * 4 + g * 2, 2)]

    sib_slot = (4 * other, 4 - 2 * other, 2 - 2 * other)
    my_slot = (4 * c, 4 - 2 * c, 2 - 2 * c)

    def kv_way(n, g, src, dst, where):
        return remote(src, dst, k_ssem.at[n * 2 + g], k_rsem.at[n * 2 + g], where)

    def transit(g):
        return kv_via.at[pl.ds(g * 2, 2)]

    def kv_start(g):
        src = kv_own.at[pl.ds(g * 2, 2)]

        @pl.when(y >= 2)
        def _():
            kv_way(5, g, src, transit(g), at_z(1)).start()

        @pl.when(y <= 2)
        def _():
            kv_way(0, g, src, kv(3, g), at_y(1)).start()

        kv_way(2, g, src, kv(sib_slot[0], g), sibling).start()
        copy_here(src, kv_out.at[pl.ds(20 + g * 2, 2)])

    def kv_transit(g):
        @pl.when(y >= 2)
        def _():
            landed(transit(g), k_rsem.at[10 + g])
            kv_way(6, g, transit(g), kv(1, g), at_y(2)).start()

        @pl.when(y == 3)
        def _():
            kv_way(0, g, transit(g), kv(3, g), at_y(1)).start()

    passes = jnp.logical_or(y == 1, y == 2)

    def kv_first(g):
        landed(kv(3, g), k_rsem.at[g])

        @pl.when(passes)
        def _():
            kv_way(1, g, kv(3, g), kv(1, g), at_y(1)).start()

        kv_way(3, g, kv(3, g), kv(sib_slot[1], g), sibling).start()

    def kv_second(g):
        @pl.when(y >= 2)
        def _():
            landed(kv(1, g), k_rsem.at[2 + g])

        @pl.when(y <= 1)
        def _():
            landed(kv(1, g), k_rsem.at[12 + g])

        kv_way(4, g, kv(1, g), kv(sib_slot[2], g), sibling).start()

    def kv_drain(g):
        own = kv_own.at[pl.ds(g * 2, 2)]
        kv_way(0, g, own, kv(3, g), sibling).wait_send()
        for n in (2, 3, 4):
            kv_way(n, g, own, kv(3, g), sibling).wait_send()

        @pl.when(passes)
        def _():
            kv_way(1, g, own, kv(3, g), sibling).wait_send()

        @pl.when(y >= 2)
        def _():
            kv_way(5, g, own, kv(3, g), sibling).wait_send()
            kv_way(6, g, own, kv(3, g), sibling).wait_send()

    steps = {
        "W": turn_weights, "g1": gather.first, "g2": gather.second, "g3": gather.third, "sy": stage_y, "sc": stage_core,
        "sr": stage_reduce, "er": stage_relay, "se": stage_end,
        "sz": stage_z, "sp": stage_spread, "sf": stage_far, "kt": kv_transit, "k1": kv_first, "k2": kv_second,
        "rot": lambda _: rotary_tables(), "kv": kv_start, "fin": finish, "q": queries, "gs": lambda _: gather.start(2, 4),
        "M": lambda i: multiply(
            (l * 2 + x // 2, l * 2 + 1 - x // 2, (1 - l) * 2 + x // 2, (1 - l) * 2 + 1 - x // 2)[i % 4], i // 4, i % 4 == 0
        ),
    }
    groups = {"W": "mm", "M": "mm", "rot": "mm", "fin": "mm", "q": "mm", "g1": "gather", "gs": "gather", "g2": "gather", "g3": "gather",
              "kv": "kv", "kt": "kv", "k1": "kv", "k2": "kv"}
    for name, arg in SCHED:
        if groups.get(name, "prefix") in ON:
            steps[name](arg)
    if "prefix" in ON:
        for i in range(2):
            item = other + 2 * i
            for d in range(4):
                for h in range(4):
                    landed(quarter(item, (y + d) % 4, h), r_rsem.at[(i * 4 + d) * 4 + h])
    if "kv" in ON:
        for n in range(3):
            for g in range(2):
                landed(kv(my_slot[n], g), k_rsem.at[4 + 2 * n + g])
    gather.drain()
    for cp in pending:
        cp.wait_send()
    if "kv" in ON:
        for g in range(2):
            kv_drain(g)
    if "prefix" in ON:
        for h in range(4):
            end_drain(h)
    for cp in local[5 + (4 if "prefix" in ON else 0):]:
        cp.wait()


def kernel_attend(
    owner_s, len_s, order_s, pref_s, len_ref, order_ref, pref_ref, q_ref, kv_ref, f_ref, out_ref, acc, meta, work, item_of
):
    base = lax.axis_index("seq") * TOK
    seen = jnp.int32(0)
    for p in range(4):
        o = owner_s[p]
        inner = jnp.logical_and(o != 0, o != 31)
        item_of[p] = jnp.where(o == 0, 0, jnp.where(o == 31, 1, 2 + jnp.minimum(seen, 1)))
        seen = seen + inner.astype(jnp.int32)

    def look(r, carry):
        at = carry[0]
        req = order_s[r]
        stop = at + len_s[req]
        bit = jnp.int32(1) << pref_s[req]
        out = [stop]
        for rb in range(4):
            lo = base + rb * 128
            hit = jnp.logical_and(at < lo + 128, stop > lo)
            out.append(jnp.where(hit, carry[1 + 2 * rb] | bit, carry[1 + 2 * rb]))
            out.append(jnp.where(jnp.logical_and(at <= lo, stop > lo), at, carry[2 + 2 * rb]))
        return tuple(out)

    zero = jnp.int32(0)
    found = lax.fori_loop(0, REQS, look, (zero,) * 9)
    count = jnp.int32(0)
    for rb in range(4):
        for p in range(4):
            work[count] = rb * 4 + p
            count = count + ((found[1 + 2 * rb] >> p) & 1)

    first, stop, prefix = slot_tables(len_ref[...], order_ref[...], pref_ref[...])
    for rb in range(4):
        tok = (lax.broadcasted_iota(jnp.int32, (1, 256), 1) % 128 + (base + rb * 128)).astype(F32)
        begin = jnp.max(jnp.where(stop <= tok, jnp.broadcast_to(stop, (REQS, 256)), 0.0), axis=0, keepdims=True)
        inside = jnp.logical_and(first <= tok, tok < stop)
        pref = jnp.sum(jnp.where(inside, jnp.broadcast_to(prefix, (REQS, 256)), 0.0), axis=0, keepdims=True)
        meta[rb, 0:1, :] = tok
        meta[rb, 1:2, :] = begin
        meta[rb, 2:3, :] = pref
    c1 = float(QSCALE ** -0.5 / SOFTCAP)
    c2 = float(SOFTCAP * math.log2(math.e))
    ones = jnp.ones((16, KEYS), BF16)

    def queries(rb):
        lanes = pl.ds(pl.multiple_of(rb * 128, 128), 128)
        return jnp.concatenate([q_ref[0:128, lanes], q_ref[128:256, lanes]], axis=1)

    def weigh(k2, qt):
        sc = jnp.dot(k2, qt, preferred_element_type=F32)
        return jnp.exp2(jnp.tanh(sc * c1) * c2)

    for rb in range(4):
        qt = queries(rb)
        tok = meta[rb, 0:1, :]
        begin = meta[rb, 1:2, :]
        acc[rb] = jnp.zeros((144, 256), F32)
        chunks = (base + (rb + 1) * 128 - found[2 + 2 * rb] + KEYS - 1) // KEYS

        @pl.loop(0, chunks)
        def _(n):
            u = 20 + rb + 1 - (n + 1) * (KEYS // 128)
            k2 = jnp.concatenate([kv_ref[u + e, 0:128, :] for e in range(KEYS // 128)], axis=0)
            v2 = jnp.concatenate([kv_ref[u + e, 128:256, :] for e in range(KEYS // 128)], axis=1)
            key = (lax.broadcasted_iota(jnp.int32, (KEYS, 1), 0) + (base - 2560 + u * 128)).astype(F32)
            ok = jnp.logical_and(key <= tok, key >= begin)
            w = jnp.where(ok, weigh(k2, qt), 0.0).astype(BF16)
            acc[rb] += jnp.dot(jnp.concatenate([v2, ones], axis=0), w, preferred_element_type=F32)

    @pl.loop(0, count)
    def _(i):
        code = work[i]
        rb, p = code >> 2, code & 3
        item = item_of[p]
        qt = queries(rb)
        ws = []
        vs = []
        for n in range(PREFIX // KEYS):
            u = n * (KEYS // 32)
            k2 = jnp.concatenate([f_ref[item, u + 4 * (e // 2) + e % 2] for e in range(KEYS // 64)], axis=0)
            vs += [
                jnp.concatenate([f_ref[item, u + 4 * e + 2], f_ref[item, u + 4 * e + 3]], axis=0) for e in range(KEYS // 128)
            ]
            ws.append(weigh(k2, qt).astype(BF16))
        v2 = jnp.concatenate([jnp.concatenate(vs, axis=1), jnp.ones((16, PREFIX), BF16)], axis=0)
        part = jnp.dot(v2, jnp.concatenate(ws, axis=0), preferred_element_type=F32)
        acc[rb] += jnp.where(meta[rb, 2:3, :] == p.astype(F32), part, 0.0)

    for rb in range(4):
        lanes = slice(rb * 128, rb * 128 + 128)
        att = acc[rb, 0:128, :] / acc[rb, 128:129, :]
        out_ref[0:128, lanes] = att[:, 0:128].astype(BF16)
        out_ref[128:256, lanes] = att[:, 128:256].astype(BF16)


def kernel_out(
    att_ref, wo_hbm, h_ref, gain_ref, out_ref, g_buf, wo_buf, acc, gcol, sums, g_ssem, g_rsem, q_ssem, q_rsem, local_sem
):
    s = lax.axis_index("seq")
    t = lax.axis_index("tp")
    l, x = t // 4, t % 4
    gather = Gather(OUT_PIECES, False, att_ref, g_buf, g_ssem, g_rsem, 256, x, l)

    def peer(d):
        return {"tp": (t + d) % 8}

    barrier = pltpu.get_barrier_semaphore()
    for d in range(1, 8):
        pl.semaphore_signal(barrier, inc=1, device_id=peer(d), device_id_type=MESH)
    wo_copy = pltpu.make_async_copy(wo_hbm, wo_buf, local_sem.at[0])
    own_copy = pltpu.make_async_copy(att_ref, g_buf.at[pl.ds(pl.multiple_of(t * 256, 256), 256)], local_sem.at[1])
    wo_copy.start()
    own_copy.start()
    pl.semaphore_wait(barrier, 7)
    gather.start(0, 4)

    g5 = gain_ref[t]
    for b in range(5):
        gcol[b * 128:(b + 1) * 128, :] = jnp.broadcast_to(g5[b:b + 1, :], (128, 128)).T
    wo_copy.wait()
    own_copy.wait()

    def multiply(dx, dl, begin):
        shard = ((l + dl) % 2) * 4 + (x + dx) % 4
        rows = pl.ds(pl.multiple_of(shard * 256, 256), 256)

        @pl.loop(0, 4)
        def _(m):
            mm = pl.ds(pl.multiple_of(m * 144, 16), 144)
            part = jnp.dot(wo_buf[mm, rows], g_buf[rows, :], preferred_element_type=F32)
            acc[mm, :] = part if begin else acc[mm, :] + part

    multiply(0, 0, True)
    for k in range(4):
        gather.first(k)
    multiply(1, 0, False)
    multiply(3, 0, False)
    multiply(0, 1, False)
    for k in range(4):
        gather.second(k)
    multiply(2, 0, False)
    multiply(1, 1, False)
    multiply(3, 1, False)
    for k in range(4):
        gather.third(k)
    multiply(2, 1, False)

    tot = jnp.zeros((8, TOK), F32)
    for b in range(72):
        v = acc[b * 8:(b + 1) * 8, :]
        tot = tot + v * v
    sums[t] = jnp.sum(tot, axis=0, keepdims=True)
    copies = []
    for d in range(1, 8):
        cp = remote(sums.at[t], sums.at[t], q_ssem.at[d - 1], q_rsem.at[7 - d], peer(d))
        cp.start()
        copies.append(cp)
    for d in range(1, 8):
        here = sums.at[(t + d) % 8]
        remote(here, here, q_ssem.at[0], q_rsem.at[d - 1], peer(1)).wait_recv()
    tot = sums[0]
    for d in range(1, 8):
        tot = tot + sums[d]
    scale = lax.rsqrt(tot * (1.0 / WIDTH) + EPS)
    for b in range(9):
        rows = slice(b * 64, b * 64 + 64)
        g = gcol[rows, :]
        for n in range(4):
            cols = slice(n * 128, n * 128 + 128)
            post = acc[rows, cols] * scale[:, cols] * g
            out_ref[rows, cols] = (h_ref[rows, cols].astype(F32) + post).astype(BF16)
    gather.drain()
    for cp in copies:
        cp.wait_send()


def on_device(
    hidden_in, pre_gain, post_gain, w_query, key_weight, value_weight, w_out, cache, suffix_len, request_order,
    request_prefix, prefix_owner,
):
    hbm = pl.BlockSpec(memory_space=pltpu.MemorySpace.HBM)
    vmem = pl.BlockSpec(memory_space=pltpu.VMEM)
    smem = pl.BlockSpec(memory_space=pltpu.SMEM)
    dma = pltpu.SemaphoreType.DMA
    h_t = hidden_in.T
    len_row = suffix_len.reshape(1, REQS)
    order_row = request_order.reshape(1, REQS)
    pref_row = request_prefix.reshape(1, REQS)
    freq = jnp.asarray((10000.0 ** (-2.0 * np.arange(64) / HEAD)).astype(np.float32).reshape(64, 1))
    n = len(IN_PIECES)
    sends = 7 * n
    part = [
        pltpu.VMEM((4, 4, 64, 128), BF16), pltpu.VMEM((4, 64, 128), BF16), pltpu.VMEM((2, 4, 64, 128), BF16),
        pltpu.VMEM((4, 64, 128), BF16), pltpu.VMEM((4, 64, 128), BF16), pltpu.VMEM((3, 64, 128), BF16),
    ]
    q, kv, spread = pl.pallas_call(
        kernel_in,
        out_shape=(
            jax.ShapeDtypeStruct((256, TOK), BF16),
            jax.ShapeDtypeStruct((24, 256, 128), BF16),
            jax.ShapeDtypeStruct((4, 64, 64, 128), BF16),
        ),
        in_specs=[smem, vmem, vmem, vmem, vmem, vmem, hbm, hbm, hbm, hbm, hbm],
        out_specs=(vmem, vmem, vmem),
        scratch_shapes=[
            pltpu.VMEM((WIDTH, TOK), BF16),
            pltpu.VMEM((WIDTH, 512), BF16),
            pltpu.VMEM((512, WIDTH), BF16),
            pltpu.VMEM((512, TOK), F32),
            pltpu.VMEM((8, TOK), F32),
            pltpu.VMEM((64, TOK), F32),
            pltpu.VMEM((64, TOK), F32),
            pltpu.VMEM((4096, 128), BF16),
            pltpu.VMEM((64, 64, 128), BF16),
            *(part * 4),
            pltpu.VMEM((4, 256, 128), BF16), pltpu.VMEM((4, 256, 128), BF16),
            dma((sends,)), dma((8 * n,)), dma((12,)), dma((12,)), dma((4,)), dma((4,)), dma((24,)), dma((24,)),
            dma((24,)), dma((24,)), dma((8,)), dma((4,)), dma((4,)), dma((32,)), dma((32,)), dma((14,)), dma((14,)), dma((16,)),
        ],
        compiler_params=pltpu.CompilerParams(collective_id=0, has_side_effects=True, vmem_limit_bytes=34 << 20),
    )(
        *(
            pltpu.with_memory_space_constraint(a, pltpu.MemorySpace.HBM)
            for a in (
                prefix_owner, len_row, order_row, pref_row, pre_gain.reshape(36, 128), freq,
                h_t, w_query, key_weight, value_weight, cache.reshape(4096, 128),
            )
        )
    )
    att = pl.pallas_call(
        kernel_attend,
        out_shape=jax.ShapeDtypeStruct((256, TOK), BF16),
        in_specs=[smem] * 4 + [vmem] * 6,
        out_specs=vmem,
        scratch_shapes=[
            pltpu.VMEM((4, 144, 256), F32),
            pltpu.VMEM((4, 8, 256), F32),
            pltpu.SMEM((17,), jnp.int32),
            pltpu.SMEM((4,), jnp.int32),
        ],
        compiler_params=pltpu.CompilerParams(vmem_limit_bytes=16 << 20),
    )(prefix_owner, suffix_len, request_order, request_prefix, len_row, order_row, pref_row, q, kv, spread)
    gains = jnp.pad(post_gain.reshape(8, SHARD), ((0, 0), (0, 64))).reshape(8, 5, 128)
    out = pl.pallas_call(
        kernel_out,
        out_shape=jax.ShapeDtypeStruct((SHARD, TOK), BF16),
        in_specs=[vmem, hbm, vmem, vmem],
        out_specs=vmem,
        scratch_shapes=[
            pltpu.VMEM((2048, TOK), BF16),
            pltpu.VMEM((SHARD, 2048), BF16),
            pltpu.VMEM((SHARD, TOK), F32),
            pltpu.VMEM((640, 128), F32),
            pltpu.VMEM((8, 1, TOK), F32),
            dma((7 * len(OUT_PIECES),)), dma((8 * len(OUT_PIECES),)), dma((7,)), dma((7,)), dma((2,)),
        ],
        compiler_params=pltpu.CompilerParams(collective_id=1, has_side_effects=True, vmem_limit_bytes=16 << 20),
    )(att, w_out.T, h_t, gains)
    return out.T


def solution(mesh):
    placed = (
        P("seq", "tp"), P(), P(), P(None, "tp"), P(None, "tp"), P(None, "tp"), P(None, "tp"), P("seq", None, "tp"),
        P(), P(), P(), P(),
    )
    return jax.shard_map(on_device, mesh=mesh, in_specs=placed, out_specs=P("seq", "tp"), check_vma=False)
```

```python
import math

import jax
import jax.numpy as jnp
import numpy as np
from jax import lax
from jax.experimental import pallas as pl
from jax.experimental.pallas import tpu as pltpu
from jax.sharding import PartitionSpec as P

MESH = pl.DeviceIdType.MESH
WIDTH = 4608
HEAD = 128
QSCALE = 144
PREFIX = 2048
TOK = 512
REQS = 48
SHARD = 576
IN_PIECES = (("P", "R"), ("P", "L"), ("P", "R"), ("P", "L"))
OUT_PIECES = (("P", "R"), ("P", "L"), ("Q", "R"), ("Q", "L"))
SOFTCAP = 50.0
EPS = 1e-6
KEYS = 512
ON = ("mm", "gather", "prefix", "kv")
SCHED = (
    ("W", 0), ("g1", 0), ("g1", 1), ("gs", 0), ("sy", 0), ("sc", 0), ("W", 1), ("sy", 1), ("g2", 0),
    ("sc", 1), ("W", 2), ("er", 0), ("sy", 2), ("sr", 0), ("g2", 1), ("sc", 2), ("W", 3), ("er", 1),
    ("sy", 3), ("sr", 1), ("g1", 2), ("sc", 3), ("M", 0), ("er", 2), ("se", 0), ("sz", 0), ("sr", 2),
    ("g1", 3), ("rot", 0), ("er", 3), ("se", 1), ("sz", 1), ("sr", 3), ("M", 1), ("M", 2), ("g3", 0),
    ("g3", 1), ("sp", 0), ("se", 2), ("sz", 2), ("M", 3), ("fin", 0), ("kv", 0), ("q", 0), ("se", 3),
    ("sz", 3), ("sp", 1), ("sf", 0), ("g2", 2), ("M", 4), ("g2", 3), ("sp", 2), ("sf", 1), ("M", 5),
    ("M", 6), ("sp", 3), ("kt", 0), ("g3", 2), ("g3", 3), ("M", 7), ("fin", 1), ("kv", 1), ("k1", 0),
    ("sf", 2), ("sf", 3), ("q", 1), ("kt", 1), ("k2", 0), ("k1", 1), ("k2", 1),
)
F32 = jnp.float32
BF16 = jnp.bfloat16


def remote(src, dst, ssem, rsem, where):
    return pltpu.make_async_remote_copy(
        src_ref=src, dst_ref=dst, send_sem=ssem, recv_sem=rsem, device_id=where, device_id_type=MESH
    )


class Gather:
    def __init__(self, pieces, halves, own, buf, ssem, rsem, rows, x, l):
        self.pieces = pieces
        self.own, self.buf, self.ssem, self.rsem, self.rows = own, buf, ssem, rsem, rows
        self.x, self.l = x, l
        self.count = 0
        self.started = []
        self.n = len(pieces)
        self.prow = rows // 2 if halves else rows // self.n
        self.halves = halves

    def target(self, way):
        x, l = self.x, self.l
        if way == "R":
            return {"tp": l * 4 + (x + 1) % 4}
        if way == "L":
            return {"tp": l * 4 + (x + 3) % 4}
        return {"tp": (1 - l) * 4 + x}

    def place(self, dx, dl, k):
        shard = ((self.l + dl) % 2) * 4 + (self.x + dx) % 4
        return self.part(self.buf, shard * self.rows, k)

    def part(self, ref, base, k):
        if not self.halves:
            return ref.at[pl.ds(pl.multiple_of(base + k * self.prow, 16), self.prow)]
        rows = pl.ds(pl.multiple_of(base + (k % 2) * self.prow, 16), self.prow)
        return ref.at[rows, pl.ds((k // 2) * (TOK // 2), TOK // 2)]

    def send(self, dx, dl, k, way):
        src = self.place(dx, dl, k)
        if dx == 0 and dl == 0:
            src = self.part(self.own, 0, k)
        rdx, rdl = dx, dl
        if way == "R":
            rdx = (dx + 3) % 4
        elif way == "L":
            rdx = (dx + 1) % 4
        else:
            rdl = 1 - dl
        copy = remote(
            src, self.place(dx, dl, k), self.ssem.at[self.count], self.rsem.at[(rdl * 4 + rdx) * self.n + k], self.target(way)
        )
        copy.start()
        self.count += 1
        self.started.append(copy)

    def wait(self, dx, dl, k):
        here = self.place(dx, dl, k)
        remote(here, here, self.ssem.at[0], self.rsem.at[(dl * 4 + dx) * self.n + k], self.target("R")).wait_recv()

    def start(self, k0, k1):
        for k in range(k0, k1):
            for way in ("R", "L", "Z"):
                self.send(0, 0, k, way)

    def first(self, k):
        kind, way = self.pieces[k]
        self.wait(3, 0, k)
        if way == "R":
            self.send(3, 0, k, "R")
        if kind == "Q":
            self.send(3, 0, k, "Z")
        self.wait(1, 0, k)
        if way == "L":
            self.send(1, 0, k, "L")
        if kind == "Q":
            self.send(1, 0, k, "Z")
        self.wait(0, 1, k)
        if kind == "P":
            self.send(0, 1, k, "R")
            self.send(0, 1, k, "L")

    def second(self, k):
        kind, way = self.pieces[k]
        self.wait(2, 0, k)
        if kind == "Q":
            self.send(2, 0, k, "Z")
        self.wait(3, 1, k)
        if kind == "P" and way == "R":
            self.send(3, 1, k, "R")
        self.wait(1, 1, k)
        if kind == "P" and way == "L":
            self.send(1, 1, k, "L")

    def third(self, k):
        self.wait(2, 1, k)

    def drain(self):
        for copy in self.started:
            copy.wait_send()


def slot_tables(len_row, order_row, prefix_row):
    len_row, order_row, prefix_row = (v.astype(F32) for v in (len_row, order_row, prefix_row))
    a = lax.broadcasted_iota(jnp.int32, (REQS, REQS), 0)
    b = lax.broadcasted_iota(jnp.int32, (REQS, REQS), 1)
    order_col = jnp.sum(jnp.where(a == b, jnp.broadcast_to(order_row, (REQS, REQS)), 0.0), axis=1, keepdims=True)
    chosen = order_col == b.astype(F32)
    length = jnp.sum(jnp.where(chosen, jnp.broadcast_to(len_row, (REQS, REQS)), 0.0), axis=1, keepdims=True)
    prefix = jnp.sum(jnp.where(chosen, jnp.broadcast_to(prefix_row, (REQS, REQS)), 0.0), axis=1, keepdims=True)
    length_row = jnp.sum(jnp.where(a == b, jnp.broadcast_to(length, (REQS, REQS)), 0.0), axis=0, keepdims=True)
    stop = jnp.sum(jnp.where(b <= a, jnp.broadcast_to(length_row, (REQS, REQS)), 0.0), axis=1, keepdims=True)
    return stop - length, stop, prefix


def kernel_in(*refs):
    (
        owner_ref, len_ref, order_ref, pref_ref, gain_ref, freq_ref, h_hbm, wq_hbm, wk_hbm, wv_hbm, cache_hbm,
        q_out, kv_out, f_out, h_buf, w_buf, wt, acc, sq, cos_buf, sin_buf, cache_buf, cache_f,
    ) = refs[:23]
    parts = refs[23:47]
    (
        kv_own, kv_via, g_ssem, g_rsem, y_ssem, y_rsem, b_ssem, b_rsem, z_ssem, z_rsem, t_ssem, t_rsem,
        a_ssem, a_rsem, e_sem, r_ssem, r_rsem, k_ssem, k_rsem, local_sem,
    ) = refs[47:]
    s = lax.axis_index("seq")
    t = lax.axis_index("tp")
    zh, y, c = s // 8, (s // 2) % 4, s % 2
    l, x = t // 4, t % 4
    other = 1 - c
    sibling = {"seq": zh * 8 + y * 2 + other}

    def at_y(d):
        return {"seq": zh * 8 + ((y + d) % 4) * 2 + c}

    def at_z(d):
        return {"seq": ((zh + d) % 4) * 8 + y * 2 + c}

    gather = Gather(IN_PIECES, True, h_hbm, h_buf, g_ssem, g_rsem, SHARD, x, l)

    barrier = pltpu.get_barrier_semaphore()
    peers = [gather.target("R"), gather.target("L"), gather.target("Z"), sibling]
    peers += [at_y(1), at_y(2), at_y(3), at_z(1), at_z(2), at_z(3)]
    for peer in peers:
        pl.semaphore_signal(barrier, inc=1, device_id=peer, device_id_type=MESH)

    local = []

    def copy_here(src, dst):
        cp = pltpu.make_async_copy(src, dst, local_sem.at[len(local)])
        cp.start()
        local.append(cp)
        return cp

    cache_copy = copy_here(cache_hbm, cache_buf)
    weights = [
        copy_here(wq_hbm, w_buf.at[:, pl.ds(0, 256)]),
        copy_here(wk_hbm, w_buf.at[:, pl.ds(256, 128)]),
        copy_here(wv_hbm, w_buf.at[:, pl.ds(384, 128)]),
        copy_here(h_hbm, h_buf.at[pl.ds(pl.multiple_of(t * SHARD, 16), SHARD)]),
    ]
    pl.semaphore_wait(barrier, len(peers))
    if "gather" in ON:
        gather.start(0, 2)

    to = lax.broadcasted_iota(jnp.int32, (256, 256), 0)
    of = lax.broadcasted_iota(jnp.int32, (256, 256), 1)
    apart = jnp.where(of == 2 * to - jnp.where(to < 128, 0, 255), 1.0, 0.0).astype(BF16)

    def split_cache(h):
        for j in range(4):
            b = j * 4 + h
            both = jnp.dot(apart, cache_buf[b * 256:(b + 1) * 256, :], preferred_element_type=F32)
            values = both[128:256].T.astype(BF16)
            for e in range(2):
                cache_f[b * 4 + e] = both[e * 64:e * 64 + 64].astype(BF16)
                cache_f[b * 4 + 2 + e] = values[e * 64:e * 64 + 64]

    cache_copy.wait()

    halves = [parts[h * 6:h * 6 + 5] for h in range(4)]
    zin = [parts[h * 6 + 5] for h in range(4)]
    pending = []

    def push(src, dst, ssem, rsem, where):
        cp = remote(src, dst, ssem, rsem, where)
        cp.start()
        pending.append(cp)

    def landed(ref, rsem):
        remote(ref, ref, y_ssem.at[0], rsem, sibling).wait_recv()

    own_y = []
    for h in (range(4) if "prefix" in ON else ()):
        yb = halves[h][0]
        split_cache(h)
        for d in (1, 3, 2):
            j = (y + d) % 4
            push(cache_f.at[pl.ds(j * 16 + h * 4, 4)], yb.at[y], y_ssem.at[h * 3 + d - 1], y_rsem.at[h * 3 + 3 - d], at_y(d))
        own_y.append(copy_here(cache_f.at[pl.ds(y * 16 + h * 4, 4)], yb.at[y]))

    oc = jnp.int32(-1)
    od = jnp.int32(-1)
    for p in range(4):
        o = owner_ref[p]
        inner = jnp.logical_and(o != 0, o != 31)
        fresh = oc < 0
        od = jnp.where(jnp.logical_and(inner, jnp.logical_not(fresh)), o, od)
        oc = jnp.where(jnp.logical_and(inner, fresh), o, oc)
    oc = jnp.clip(oc, 0, 31)
    od = jnp.clip(od, 0, 31)
    mine = jnp.where(c == 0, oc, od)
    theirs = jnp.where(c == 0, od, oc)

    def quarter(item, j, h):
        return f_out.at[item, pl.ds(j * 16 + h * 4, 4)]

    far = (zh - 3 * c) % 4

    def end_copy(h, d, src):
        return remote(src, quarter(c, y, h), a_ssem.at[h * 2 + d // 2], a_rsem.at[h], at_z(d))

    def stage_y(h):
        yb, sb, cb, zb, pb = halves[h]
        own_y[h].wait()
        for d in (1, 3, 2):
            landed(yb.at[(y + d) % 4], y_rsem.at[h * 3 + d - 1])
        sb[...] = yb[(theirs >> 1) & 3]
        push(sb, cb.at[c], b_ssem.at[h], b_rsem.at[h], sibling)

        @pl.when(far == 0)
        def _():
            end_copy(h, 1, yb.at[3 * c]).start()
            end_copy(h, 3, yb.at[3 * c]).start()
            pltpu.make_async_copy(yb.at[3 * c], quarter(c, y, h), e_sem.at[h]).start()

        cb[c] = yb[(mine >> 1) & 3]

    def unit(ref, d):
        return ref.at[(zh + 4 - d) % 4]

    def zsem(sem, h, n):
        return sem.at[h * 6 + n]

    def stage_core(h):
        yb, sb, cb, zb, pb = halves[h]
        landed(cb.at[other], b_rsem.at[h])
        zb[...] = cb[mine & 1]
        for d in (1, 3, 2):
            push(unit(zb, d), zin[h].at[d - 1], zsem(z_ssem, h, d - 1), zsem(z_rsem, h, d - 1), at_z(4 - d))

    zo = mine >> 3

    def stage_reduce(h):
        yb, sb, cb, zb, pb = halves[h]
        whole = zb[zh]
        for d in (1, 3, 2):
            landed(zin[h].at[d - 1], zsem(z_rsem, h, d - 1))
            whole = jnp.where(zo == (zh + d) % 4, zin[h][d - 1], whole)
        pb[zh] = whole
        for d in (1, 3, 2):
            push(unit(pb, 0), unit(pb, 0), zsem(z_ssem, h, 2 + d), zsem(z_rsem, h, 2 + d), at_z(d))

    def stage_relay(h):
        @pl.when(jnp.logical_or(far == 1, far == 3))
        def _():
            landed(quarter(c, y, h), a_rsem.at[h])

        @pl.when(far == (1 if h % 2 == 0 else 3))
        def _():
            end_copy(h, 1 if h % 2 == 0 else 3, quarter(c, y, h)).start()

    def relay(item, j, h, i, d):
        n = (i * 4 + d) * 4 + h
        push(quarter(item, j, h), quarter(item, j, h), r_ssem.at[n], r_rsem.at[n], sibling)

    def spread_own(h, i, src):
        item = c + 2 * i
        for d in (1, 3):
            push(src, quarter(item, y, h), t_ssem.at[(i * 3 + d - 1) * 4 + h], t_rsem.at[(i * 3 + 3 - d) * 4 + h], at_y(d))
        n = (i * 4) * 4 + h
        push(src, quarter(item, y, h), r_ssem.at[n], r_rsem.at[n], sibling)

    def stage_end(h):
        yb, sb, cb, zb, pb = halves[h]

        @pl.when(far == 2)
        def _():
            landed(quarter(c, y, h), a_rsem.at[h])

        @pl.when(far == 0)
        def _():
            pltpu.make_async_copy(yb.at[3 * c], quarter(c, y, h), e_sem.at[h]).wait()

        spread_own(h, 0, quarter(c, y, h))

    def stage_z(h):
        yb, sb, cb, zb, pb = halves[h]
        for d in (1, 3, 2):
            landed(unit(pb, d), zsem(z_rsem, h, 2 + d))
        copy_here(pb, quarter(c + 2, y, h))
        spread_own(h, 1, pb)

    def end_drain(h):
        @pl.when(far == 0)
        def _():
            end_copy(h, 1, quarter(c, y, h)).wait_send()
            end_copy(h, 3, quarter(c, y, h)).wait_send()

        @pl.when(far == (1 if h % 2 == 0 else 3))
        def _():
            end_copy(h, 1 if h % 2 == 0 else 3, quarter(c, y, h)).wait_send()

    def stage_spread(h):
        for i in range(2):
            item = c + 2 * i
            for d in (3, 1):
                j = (y + d) % 4
                landed(quarter(item, j, h), t_rsem.at[(i * 3 + d - 1) * 4 + h])
                if (i == 0 and d == 3) or (i == 1 and d == 1):
                    push(
                        quarter(item, j, h), quarter(item, j, h), t_ssem.at[(i * 3 + 1) * 4 + h], t_rsem.at[(i * 3 + 1) * 4 + h],
                        at_y(1 if i == 0 else 3),
                    )
                relay(item, j, h, i, d)

    def stage_far(h):
        for i in range(2):
            item = c + 2 * i
            j = (y + 2) % 4
            landed(quarter(item, j, h), t_rsem.at[(i * 3 + 1) * 4 + h])
            relay(item, j, h, i, 2)

    def rotary_tables():
        first, stop, _ = slot_tables(len_ref[...], order_ref[...], pref_ref[...])
        tok = (lax.broadcasted_iota(jnp.int32, (1, TOK), 1) + s * TOK).astype(F32)
        start = jnp.max(jnp.where(stop <= tok, jnp.broadcast_to(stop, (REQS, TOK)), 0.0), axis=0, keepdims=True)
        place = tok - start + float(PREFIX)
        angle = freq_ref[...] * place
        cos_buf[...] = jnp.cos(angle)
        sin_buf[...] = jnp.sin(angle)

    def turn_weights(i):
        @pl.loop(i * 9, i * 9 + 9)
        def _(f):
            rows = pl.ds(pl.multiple_of(f * 128, 128), 128)
            g = gain_ref[pl.ds(f, 1), :]
            for cb in range(4):
                w = w_buf[rows, cb * 128:(cb + 1) * 128].astype(F32).T
                wt[cb * 128:(cb + 1) * 128, rows] = (w * g).astype(BF16)

    def multiply(pair, g, begin):
        rows = pl.multiple_of(pair * 1152, 128)
        lanes = slice(g * 256, g * 256 + 256)
        for m in range(2):
            mm = slice(m * 256, m * 256 + 256)
            part = jnp.dot(wt[mm, pl.ds(rows, 1152)], h_buf[pl.ds(rows, 1152), lanes], preferred_element_type=F32)
            acc[mm, lanes] = part if begin else acc[mm, lanes] + part

        @pl.loop(0, 9)
        def _(b):
            v = h_buf[pl.ds(pl.multiple_of(rows + b * 128, 128), 128), lanes].astype(F32)
            v = v * v
            tot = v[0:8]
            for e in range(1, 16):
                tot = tot + v[e * 8:(e + 1) * 8]
            sq[:, lanes] = sq[:, lanes] + tot

    sq[...] = jnp.zeros_like(sq)
    for cp in weights:
        cp.wait()

    def turned(r0, g):
        lanes = slice(g * 256, g * 256 + 256)
        scale = lax.rsqrt(jnp.sum(sq[:, lanes], axis=0, keepdims=True) * (1.0 / WIDTH) + EPS)
        cos, sin = cos_buf[:, lanes], sin_buf[:, lanes]
        a = acc[r0:r0 + 64, lanes] * scale
        b = acc[r0 + 64:r0 + 128, lanes] * scale
        return a * cos - b * sin, b * cos + a * sin, scale

    def finish(g):
        a, b, scale = turned(256, g)
        kt = jnp.concatenate([a, b], axis=0)
        vt = (acc[384:512, g * 256:g * 256 + 256] * scale).astype(BF16)
        for e in range(2):
            kv_own[g * 2 + e, 0:128, :] = kt[:, e * 128:(e + 1) * 128].T.astype(BF16)
            kv_own[g * 2 + e, 128:256, :] = vt[:, e * 128:(e + 1) * 128]

    def queries(g):
        lanes = slice(g * 256, g * 256 + 256)
        for hd in range(2):
            a, b, _ = turned(hd * 128, g)
            q_out[hd * 128:hd * 128 + 64, lanes] = a.astype(BF16)
            q_out[hd * 128 + 64:hd * 128 + 128, lanes] = b.astype(BF16)

    def kv(slot, g):
        return kv_out.at[pl.ds(slot * 4 + g * 2, 2)]

    sib_slot = (4 * other, 4 - 2 * other, 2 - 2 * other)
    my_slot = (4 * c, 4 - 2 * c, 2 - 2 * c)

    def kv_way(n, g, src, dst, where):
        return remote(src, dst, k_ssem.at[n * 2 + g], k_rsem.at[n * 2 + g], where)

    def transit(g):
        return kv_via.at[pl.ds(g * 2, 2)]

    def kv_start(g):
        src = kv_own.at[pl.ds(g * 2, 2)]

        @pl.when(y >= 2)
        def _():
            kv_way(5, g, src, transit(g), at_z(1)).start()

        @pl.when(y <= 2)
        def _():
            kv_way(0, g, src, kv(3, g), at_y(1)).start()

        kv_way(2, g, src, kv(sib_slot[0], g), sibling).start()
        copy_here(src, kv_out.at[pl.ds(20 + g * 2, 2)])

    def kv_transit(g):
        @pl.when(y >= 2)
        def _():
            landed(transit(g), k_rsem.at[10 + g])
            kv_way(6, g, transit(g), kv(1, g), at_y(2)).start()

        @pl.when(y == 3)
        def _():
            kv_way(0, g, transit(g), kv(3, g), at_y(1)).start()

    passes = jnp.logical_or(y == 1, y == 2)

    def kv_first(g):
        landed(kv(3, g), k_rsem.at[g])

        @pl.when(passes)
        def _():
            kv_way(1, g, kv(3, g), kv(1, g), at_y(1)).start()

        kv_way(3, g, kv(3, g), kv(sib_slot[1], g), sibling).start()

    def kv_second(g):
        @pl.when(y >= 2)
        def _():
            landed(kv(1, g), k_rsem.at[2 + g])

        @pl.when(y <= 1)
        def _():
            landed(kv(1, g), k_rsem.at[12 + g])

        kv_way(4, g, kv(1, g), kv(sib_slot[2], g), sibling).start()

    def kv_drain(g):
        own = kv_own.at[pl.ds(g * 2, 2)]
        kv_way(0, g, own, kv(3, g), sibling).wait_send()
        for n in (2, 3, 4):
            kv_way(n, g, own, kv(3, g), sibling).wait_send()

        @pl.when(passes)
        def _():
            kv_way(1, g, own, kv(3, g), sibling).wait_send()

        @pl.when(y >= 2)
        def _():
            kv_way(5, g, own, kv(3, g), sibling).wait_send()
            kv_way(6, g, own, kv(3, g), sibling).wait_send()

    steps = {
        "W": turn_weights, "g1": gather.first, "g2": gather.second, "g3": gather.third, "sy": stage_y, "sc": stage_core,
        "sr": stage_reduce, "er": stage_relay, "se": stage_end,
        "sz": stage_z, "sp": stage_spread, "sf": stage_far, "kt": kv_transit, "k1": kv_first, "k2": kv_second,
        "rot": lambda _: rotary_tables(), "kv": kv_start, "fin": finish, "q": queries, "gs": lambda _: gather.start(2, 4),
        "M": lambda i: multiply(
            (l * 2 + x // 2, l * 2 + 1 - x // 2, (1 - l) * 2 + x // 2, (1 - l) * 2 + 1 - x // 2)[i % 4], i // 4, i % 4 == 0
        ),
    }
    groups = {"W": "mm", "M": "mm", "rot": "mm", "fin": "mm", "q": "mm", "g1": "gather", "gs": "gather", "g2": "gather", "g3": "gather",
              "kv": "kv", "kt": "kv", "k1": "kv", "k2": "kv"}
    for name, arg in SCHED:
        if groups.get(name, "prefix") in ON:
            steps[name](arg)
    if "prefix" in ON:
        for i in range(2):
            item = other + 2 * i
            for d in range(4):
                for h in range(4):
                    landed(quarter(item, (y + d) % 4, h), r_rsem.at[(i * 4 + d) * 4 + h])
    if "kv" in ON:
        for n in range(3):
            for g in range(2):
                landed(kv(my_slot[n], g), k_rsem.at[4 + 2 * n + g])
    gather.drain()
    for cp in pending:
        cp.wait_send()
    if "kv" in ON:
        for g in range(2):
            kv_drain(g)
    if "prefix" in ON:
        for h in range(4):
            end_drain(h)
    for cp in local[5 + (4 if "prefix" in ON else 0):]:
        cp.wait()


def kernel_attend(
    owner_s, len_s, order_s, pref_s, len_ref, order_ref, pref_ref, q_ref, kv_ref, f_ref, out_ref, acc, meta, work, item_of
):
    base = lax.axis_index("seq") * TOK
    seen = jnp.int32(0)
    for p in range(4):
        o = owner_s[p]
        inner = jnp.logical_and(o != 0, o != 31)
        item_of[p] = jnp.where(o == 0, 0, jnp.where(o == 31, 1, 2 + jnp.minimum(seen, 1)))
        seen = seen + inner.astype(jnp.int32)

    def look(r, carry):
        at = carry[0]
        req = order_s[r]
        stop = at + len_s[req]
        bit = jnp.int32(1) << pref_s[req]
        out = [stop]
        for rb in range(4):
            lo = base + rb * 128
            hit = jnp.logical_and(at < lo + 128, stop > lo)
            out.append(jnp.where(hit, carry[1 + 2 * rb] | bit, carry[1 + 2 * rb]))
            out.append(jnp.where(jnp.logical_and(at <= lo, stop > lo), at, carry[2 + 2 * rb]))
        return tuple(out)

    zero = jnp.int32(0)
    found = lax.fori_loop(0, REQS, look, (zero,) * 9)
    count = jnp.int32(0)
    for rb in range(4):
        for p in range(4):
            work[count] = rb * 4 + p
            count = count + ((found[1 + 2 * rb] >> p) & 1)

    first, stop, prefix = slot_tables(len_ref[...], order_ref[...], pref_ref[...])
    for rb in range(4):
        tok = (lax.broadcasted_iota(jnp.int32, (1, 256), 1) % 128 + (base + rb * 128)).astype(F32)
        begin = jnp.max(jnp.where(stop <= tok, jnp.broadcast_to(stop, (REQS, 256)), 0.0), axis=0, keepdims=True)
        inside = jnp.logical_and(first <= tok, tok < stop)
        pref = jnp.sum(jnp.where(inside, jnp.broadcast_to(prefix, (REQS, 256)), 0.0), axis=0, keepdims=True)
        meta[rb, 0:1, :] = tok
        meta[rb, 1:2, :] = begin
        meta[rb, 2:3, :] = pref
    c1 = float(QSCALE ** -0.5 / SOFTCAP)
    c2 = float(SOFTCAP * math.log2(math.e))
    ones = jnp.ones((16, KEYS), BF16)

    def queries(rb):
        lanes = pl.ds(pl.multiple_of(rb * 128, 128), 128)
        return jnp.concatenate([q_ref[0:128, lanes], q_ref[128:256, lanes]], axis=1)

    def weigh(k2, qt):
        sc = jnp.dot(k2, qt, preferred_element_type=F32)
        return jnp.exp2(jnp.tanh(sc * c1) * c2)

    for rb in range(4):
        qt = queries(rb)
        tok = meta[rb, 0:1, :]
        begin = meta[rb, 1:2, :]
        acc[rb] = jnp.zeros((144, 256), F32)
        chunks = (base + (rb + 1) * 128 - found[2 + 2 * rb] + KEYS - 1) // KEYS

        @pl.loop(0, chunks)
        def _(n):
            u = 20 + rb + 1 - (n + 1) * (KEYS // 128)
            k2 = jnp.concatenate([kv_ref[u + e, 0:128, :] for e in range(KEYS // 128)], axis=0)
            v2 = jnp.concatenate([kv_ref[u + e, 128:256, :] for e in range(KEYS // 128)], axis=1)
            key = (lax.broadcasted_iota(jnp.int32, (KEYS, 1), 0) + (base - 2560 + u * 128)).astype(F32)
            ok = jnp.logical_and(key <= tok, key >= begin)
            w = jnp.where(ok, weigh(k2, qt), 0.0).astype(BF16)
            acc[rb] += jnp.dot(jnp.concatenate([v2, ones], axis=0), w, preferred_element_type=F32)

    @pl.loop(0, count)
    def _(i):
        code = work[i]
        rb, p = code >> 2, code & 3
        item = item_of[p]
        qt = queries(rb)
        ws = []
        vs = []
        for n in range(PREFIX // KEYS):
            u = n * (KEYS // 32)
            k2 = jnp.concatenate([f_ref[item, u + 4 * (e // 2) + e % 2] for e in range(KEYS // 64)], axis=0)
            vs += [
                jnp.concatenate([f_ref[item, u + 4 * e + 2], f_ref[item, u + 4 * e + 3]], axis=0) for e in range(KEYS // 128)
            ]
            ws.append(weigh(k2, qt).astype(BF16))
        v2 = jnp.concatenate([jnp.concatenate(vs, axis=1), jnp.ones((16, PREFIX), BF16)], axis=0)
        part = jnp.dot(v2, jnp.concatenate(ws, axis=0), preferred_element_type=F32)
        acc[rb] += jnp.where(meta[rb, 2:3, :] == p.astype(F32), part, 0.0)

    for rb in range(4):
        lanes = slice(rb * 128, rb * 128 + 128)
        att = acc[rb, 0:128, :] / acc[rb, 128:129, :]
        out_ref[0:128, lanes] = att[:, 0:128].astype(BF16)
        out_ref[128:256, lanes] = att[:, 128:256].astype(BF16)


def kernel_out(
    att_ref, wo_hbm, h_ref, gain_ref, out_ref, g_buf, wo_buf, acc, gcol, sums, g_ssem, g_rsem, q_ssem, q_rsem, local_sem
):
    s = lax.axis_index("seq")
    t = lax.axis_index("tp")
    l, x = t // 4, t % 4
    gather = Gather(OUT_PIECES, False, att_ref, g_buf, g_ssem, g_rsem, 256, x, l)

    def peer(d):
        return {"tp": (t + d) % 8}

    barrier = pltpu.get_barrier_semaphore()
    for d in range(1, 8):
        pl.semaphore_signal(barrier, inc=1, device_id=peer(d), device_id_type=MESH)
    wo_copy = pltpu.make_async_copy(wo_hbm, wo_buf, local_sem.at[0])
    own_copy = pltpu.make_async_copy(att_ref, g_buf.at[pl.ds(pl.multiple_of(t * 256, 256), 256)], local_sem.at[1])
    wo_copy.start()
    own_copy.start()
    pl.semaphore_wait(barrier, 7)
    gather.start(0, 4)

    g5 = gain_ref[t]
    for b in range(5):
        gcol[b * 128:(b + 1) * 128, :] = jnp.broadcast_to(g5[b:b + 1, :], (128, 128)).T
    wo_copy.wait()
    own_copy.wait()

    def multiply(dx, dl, begin):
        shard = ((l + dl) % 2) * 4 + (x + dx) % 4
        rows = pl.ds(pl.multiple_of(shard * 256, 256), 256)

        @pl.loop(0, 4)
        def _(m):
            mm = pl.ds(pl.multiple_of(m * 144, 16), 144)
            part = jnp.dot(wo_buf[mm, rows], g_buf[rows, :], preferred_element_type=F32)
            acc[mm, :] = part if begin else acc[mm, :] + part

    multiply(0, 0, True)
    for k in range(4):
        gather.first(k)
    multiply(1, 0, False)
    multiply(3, 0, False)
    multiply(0, 1, False)
    for k in range(4):
        gather.second(k)
    multiply(2, 0, False)
    multiply(1, 1, False)
    multiply(3, 1, False)
    for k in range(4):
        gather.third(k)
    multiply(2, 1, False)

    tot = jnp.zeros((8, TOK), F32)
    for b in range(72):
        v = acc[b * 8:(b + 1) * 8, :]
        tot = tot + v * v
    sums[t] = jnp.sum(tot, axis=0, keepdims=True)
    copies = []
    for d in range(1, 8):
        cp = remote(sums.at[t], sums.at[t], q_ssem.at[d - 1], q_rsem.at[7 - d], peer(d))
        cp.start()
        copies.append(cp)
    for d in range(1, 8):
        here = sums.at[(t + d) % 8]
        remote(here, here, q_ssem.at[0], q_rsem.at[d - 1], peer(1)).wait_recv()
    tot = sums[0]
    for d in range(1, 8):
        tot = tot + sums[d]
    scale = lax.rsqrt(tot * (1.0 / WIDTH) + EPS)
    for b in range(9):
        rows = slice(b * 64, b * 64 + 64)
        g = gcol[rows, :]
        for n in range(4):
            cols = slice(n * 128, n * 128 + 128)
            post = acc[rows, cols] * scale[:, cols] * g
            out_ref[rows, cols] = (h_ref[rows, cols].astype(F32) + post).astype(BF16)
    gather.drain()
    for cp in copies:
        cp.wait_send()


def on_device(
    hidden_in, pre_gain, post_gain, w_query, key_weight, value_weight, w_out, cache, suffix_len, request_order,
    request_prefix, prefix_owner,
):
    hbm = pl.BlockSpec(memory_space=pltpu.MemorySpace.HBM)
    vmem = pl.BlockSpec(memory_space=pltpu.VMEM)
    smem = pl.BlockSpec(memory_space=pltpu.SMEM)
    dma = pltpu.SemaphoreType.DMA
    h_t = hidden_in.T
    len_row = suffix_len.reshape(1, REQS)
    order_row = request_order.reshape(1, REQS)
    pref_row = request_prefix.reshape(1, REQS)
    freq = jnp.asarray((10000.0 ** (-2.0 * np.arange(64) / HEAD)).astype(np.float32).reshape(64, 1))
    n = len(IN_PIECES)
    sends = 7 * n
    part = [
        pltpu.VMEM((4, 4, 64, 128), BF16), pltpu.VMEM((4, 64, 128), BF16), pltpu.VMEM((2, 4, 64, 128), BF16),
        pltpu.VMEM((4, 64, 128), BF16), pltpu.VMEM((4, 64, 128), BF16), pltpu.VMEM((3, 64, 128), BF16),
    ]
    q, kv, spread = pl.pallas_call(
        kernel_in,
        out_shape=(
            jax.ShapeDtypeStruct((256, TOK), BF16),
            jax.ShapeDtypeStruct((24, 256, 128), BF16),
            jax.ShapeDtypeStruct((4, 64, 64, 128), BF16),
        ),
        in_specs=[smem, vmem, vmem, vmem, vmem, vmem, hbm, hbm, hbm, hbm, hbm],
        out_specs=(vmem, vmem, vmem),
        scratch_shapes=[
            pltpu.VMEM((WIDTH, TOK), BF16),
            pltpu.VMEM((WIDTH, 512), BF16),
            pltpu.VMEM((512, WIDTH), BF16),
            pltpu.VMEM((512, TOK), F32),
            pltpu.VMEM((8, TOK), F32),
            pltpu.VMEM((64, TOK), F32),
            pltpu.VMEM((64, TOK), F32),
            pltpu.VMEM((4096, 128), BF16),
            pltpu.VMEM((64, 64, 128), BF16),
            *(part * 4),
            pltpu.VMEM((4, 256, 128), BF16), pltpu.VMEM((4, 256, 128), BF16),
            dma((sends,)), dma((8 * n,)), dma((12,)), dma((12,)), dma((4,)), dma((4,)), dma((24,)), dma((24,)),
            dma((24,)), dma((24,)), dma((8,)), dma((4,)), dma((4,)), dma((32,)), dma((32,)), dma((14,)), dma((14,)), dma((16,)),
        ],
        compiler_params=pltpu.CompilerParams(collective_id=0, has_side_effects=True, vmem_limit_bytes=34 << 20),
    )(
        *(
            pltpu.with_memory_space_constraint(a, pltpu.MemorySpace.HBM)
            for a in (
                prefix_owner, len_row, order_row, pref_row, pre_gain.reshape(36, 128), freq,
                h_t, w_query, key_weight, value_weight, cache.reshape(4096, 128),
            )
        )
    )
    att = pl.pallas_call(
        kernel_attend,
        out_shape=jax.ShapeDtypeStruct((256, TOK), BF16),
        in_specs=[smem] * 4 + [vmem] * 6,
        out_specs=vmem,
        scratch_shapes=[
            pltpu.VMEM((4, 144, 256), F32),
            pltpu.VMEM((4, 8, 256), F32),
            pltpu.SMEM((17,), jnp.int32),
            pltpu.SMEM((4,), jnp.int32),
        ],
        compiler_params=pltpu.CompilerParams(vmem_limit_bytes=16 << 20),
    )(prefix_owner, suffix_len, request_order, request_prefix, len_row, order_row, pref_row, q, kv, spread)
    gains = jnp.pad(post_gain.reshape(8, SHARD), ((0, 0), (0, 64))).reshape(8, 5, 128)
    out = pl.pallas_call(
        kernel_out,
        out_shape=jax.ShapeDtypeStruct((SHARD, TOK), BF16),
        in_specs=[vmem, hbm, vmem, vmem],
        out_specs=vmem,
        scratch_shapes=[
            pltpu.VMEM((2048, TOK), BF16),
            pltpu.VMEM((SHARD, 2048), BF16),
            pltpu.VMEM((SHARD, TOK), F32),
            pltpu.VMEM((640, 128), F32),
            pltpu.VMEM((8, 1, TOK), F32),
            dma((7 * len(OUT_PIECES),)), dma((8 * len(OUT_PIECES),)), dma((7,)), dma((7,)), dma((2,)),
        ],
        compiler_params=pltpu.CompilerParams(collective_id=1, has_side_effects=True, vmem_limit_bytes=16 << 20),
    )(att, w_out.T, h_t, gains)
    return out.T


def solution(mesh):
    placed = (
        P("seq", "tp"), P(), P(), P(None, "tp"), P(None, "tp"), P(None, "tp"), P(None, "tp"), P("seq", None, "tp"),
        P(), P(), P(), P(),
    )
    return jax.shard_map(on_device, mesh=mesh, in_specs=placed, out_specs=P("seq", "tp"), check_vma=False)
```

```python
import math

import jax
import jax.numpy as jnp
import numpy as np
from jax import lax
from jax.experimental import pallas as pl
from jax.experimental.pallas import tpu as pltpu
from jax.sharding import PartitionSpec as P

MESH = pl.DeviceIdType.MESH
WIDTH = 4608
HEAD = 128
QSCALE = 144
PREFIX = 2048
TOK = 512
REQS = 48
SHARD = 576
IN_PIECES = (("P", "R"), ("P", "L")) * 4
OUT_PIECES = (("P", "R"), ("P", "L"), ("Q", "R"), ("Q", "L")) * 2
SOFTCAP = 50.0
EPS = 1e-6
KEYS = 512
ON = ("mm", "gather", "prefix", "kv")
SCHED = (
    ("W", 0), ("g1", 0), ("g1", 1), ("gs", 0), ("sy", 0), ("sc", 0), ("W", 1), ("sy", 1), ("g2", 0),
    ("sc", 1), ("W", 2), ("er", 0), ("sy", 2), ("sr", 0), ("g2", 1), ("sc", 2), ("W", 3), ("er", 1),
    ("sy", 3), ("sr", 1), ("g1", 2), ("sc", 3), ("M", 0), ("er", 2), ("se", 0), ("sz", 0), ("sr", 2),
    ("g1", 3), ("rot", 0), ("er", 3), ("se", 1), ("sz", 1), ("sr", 3), ("M", 1), ("M", 2), ("g3", 0),
    ("g3", 1), ("sp", 0), ("se", 2), ("sz", 2), ("M", 3), ("fin", 0), ("kv", 0), ("q", 0), ("se", 3),
    ("sz", 3), ("sp", 1), ("sf", 0), ("g2", 2), ("M", 4), ("g2", 3), ("sp", 2), ("sf", 1), ("M", 5),
    ("M", 6), ("sp", 3), ("kt", 0), ("g3", 2), ("g3", 3), ("M", 7), ("fin", 1), ("kv", 1), ("k1", 0),
    ("sf", 2), ("sf", 3), ("q", 1), ("kt", 1), ("k2", 0), ("k1", 1), ("k2", 1),
)
F32 = jnp.float32
BF16 = jnp.bfloat16


def remote(src, dst, ssem, rsem, where):
    return pltpu.make_async_remote_copy(
        src_ref=src, dst_ref=dst, send_sem=ssem, recv_sem=rsem, device_id=where, device_id_type=MESH
    )


class Gather:
    def __init__(self, pieces, halves, own, buf, ssem, rsem, rows, x, l):
        self.pieces = pieces
        self.own, self.buf, self.ssem, self.rsem, self.rows = own, buf, ssem, rsem, rows
        self.x, self.l = x, l
        self.count = 0
        self.started = []
        self.n = len(pieces)
        self.per = self.n // 2
        self.prow = rows // self.per if halves else rows // self.n
        self.halves = halves

    def target(self, way):
        x, l = self.x, self.l
        if way == "R":
            return {"tp": l * 4 + (x + 1) % 4}
        if way == "L":
            return {"tp": l * 4 + (x + 3) % 4}
        return {"tp": (1 - l) * 4 + x}

    def place(self, dx, dl, k):
        shard = ((self.l + dl) % 2) * 4 + (self.x + dx) % 4
        return self.part(self.buf, shard * self.rows, k)

    def part(self, ref, base, k):
        if not self.halves:
            return ref.at[pl.ds(pl.multiple_of(base + k * self.prow, 16), self.prow)]
        rows = pl.ds(pl.multiple_of(base + (k % self.per) * self.prow, 16), self.prow)
        return ref.at[rows, pl.ds((k // self.per) * (TOK // 2), TOK // 2)]

    def send(self, dx, dl, k, way):
        src = self.place(dx, dl, k)
        if dx == 0 and dl == 0:
            src = self.part(self.own, 0, k)
        rdx, rdl = dx, dl
        if way == "R":
            rdx = (dx + 3) % 4
        elif way == "L":
            rdx = (dx + 1) % 4
        else:
            rdl = 1 - dl
        copy = remote(
            src, self.place(dx, dl, k), self.ssem.at[self.count], self.rsem.at[(rdl * 4 + rdx) * self.n + k], self.target(way)
        )
        copy.start()
        self.count += 1
        self.started.append(copy)

    def wait(self, dx, dl, k):
        here = self.place(dx, dl, k)
        remote(here, here, self.ssem.at[0], self.rsem.at[(dl * 4 + dx) * self.n + k], self.target("R")).wait_recv()

    def start(self, k0, k1):
        for k in range(k0, k1):
            for way in ("R", "L", "Z"):
                self.send(0, 0, k, way)

    def first(self, k):
        kind, way = self.pieces[k]
        self.wait(3, 0, k)
        if way == "R":
            self.send(3, 0, k, "R")
        if kind == "Q":
            self.send(3, 0, k, "Z")
        self.wait(1, 0, k)
        if way == "L":
            self.send(1, 0, k, "L")
        if kind == "Q":
            self.send(1, 0, k, "Z")
        self.wait(0, 1, k)
        if kind == "P":
            self.send(0, 1, k, "R")
            self.send(0, 1, k, "L")

    def second(self, k):
        kind, way = self.pieces[k]
        self.wait(2, 0, k)
        if kind == "Q":
            self.send(2, 0, k, "Z")
        self.wait(3, 1, k)
        if kind == "P" and way == "R":
            self.send(3, 1, k, "R")
        self.wait(1, 1, k)
        if kind == "P" and way == "L":
            self.send(1, 1, k, "L")

    def third(self, k):
        self.wait(2, 1, k)

    def drain(self):
        for copy in self.started:
            copy.wait_send()


def slot_tables(len_row, order_row, prefix_row):
    len_row, order_row, prefix_row = (v.astype(F32) for v in (len_row, order_row, prefix_row))
    a = lax.broadcasted_iota(jnp.int32, (REQS, REQS), 0)
    b = lax.broadcasted_iota(jnp.int32, (REQS, REQS), 1)
    order_col = jnp.sum(jnp.where(a == b, jnp.broadcast_to(order_row, (REQS, REQS)), 0.0), axis=1, keepdims=True)
    chosen = order_col == b.astype(F32)
    length = jnp.sum(jnp.where(chosen, jnp.broadcast_to(len_row, (REQS, REQS)), 0.0), axis=1, keepdims=True)
    prefix = jnp.sum(jnp.where(chosen, jnp.broadcast_to(prefix_row, (REQS, REQS)), 0.0), axis=1, keepdims=True)
    length_row = jnp.sum(jnp.where(a == b, jnp.broadcast_to(length, (REQS, REQS)), 0.0), axis=0, keepdims=True)
    stop = jnp.sum(jnp.where(b <= a, jnp.broadcast_to(length_row, (REQS, REQS)), 0.0), axis=1, keepdims=True)
    return stop - length, stop, prefix


def kernel_in(*refs):
    (
        owner_ref, len_ref, order_ref, pref_ref, gain_ref, freq_ref, h_hbm, wq_hbm, wk_hbm, wv_hbm, cache_hbm,
        q_out, kv_out, f_out, h_buf, w_buf, wt, acc, sq, cos_buf, sin_buf, cache_buf, cache_f,
    ) = refs[:23]
    parts = refs[23:47]
    (
        kv_own, kv_via, g_ssem, g_rsem, y_ssem, y_rsem, b_ssem, b_rsem, z_ssem, z_rsem, t_ssem, t_rsem,
        a_ssem, a_rsem, e_sem, r_ssem, r_rsem, k_ssem, k_rsem, local_sem,
    ) = refs[47:]
    s = lax.axis_index("seq")
    t = lax.axis_index("tp")
    zh, y, c = s // 8, (s // 2) % 4, s % 2
    l, x = t // 4, t % 4
    other = 1 - c
    sibling = {"seq": zh * 8 + y * 2 + other}

    def at_y(d):
        return {"seq": zh * 8 + ((y + d) % 4) * 2 + c}

    def at_z(d):
        return {"seq": ((zh + d) % 4) * 8 + y * 2 + c}

    gather = Gather(IN_PIECES, True, h_hbm, h_buf, g_ssem, g_rsem, SHARD, x, l)

    barrier = pltpu.get_barrier_semaphore()
    peers = [gather.target("R"), gather.target("L"), gather.target("Z"), sibling]
    peers += [at_y(1), at_y(2), at_y(3), at_z(1), at_z(2), at_z(3)]
    for peer in peers:
        pl.semaphore_signal(barrier, inc=1, device_id=peer, device_id_type=MESH)

    local = []

    def copy_here(src, dst):
        cp = pltpu.make_async_copy(src, dst, local_sem.at[len(local)])
        cp.start()
        local.append(cp)
        return cp

    cache_copy = copy_here(cache_hbm, cache_buf)
    weights = [
        copy_here(wq_hbm, w_buf.at[:, pl.ds(0, 256)]),
        copy_here(wk_hbm, w_buf.at[:, pl.ds(256, 128)]),
        copy_here(wv_hbm, w_buf.at[:, pl.ds(384, 128)]),
        copy_here(h_hbm, h_buf.at[pl.ds(pl.multiple_of(t * SHARD, 16), SHARD)]),
    ]
    pl.semaphore_wait(barrier, len(peers))
    if "gather" in ON:
        gather.start(0, 4)

    to = lax.broadcasted_iota(jnp.int32, (256, 256), 0)
    of = lax.broadcasted_iota(jnp.int32, (256, 256), 1)
    apart = jnp.where(of == 2 * to - jnp.where(to < 128, 0, 255), 1.0, 0.0).astype(BF16)

    def split_cache(h):
        for j in range(4):
            b = j * 4 + h
            both = jnp.dot(apart, cache_buf[b * 256:(b + 1) * 256, :], preferred_element_type=F32)
            values = both[128:256].T.astype(BF16)
            for e in range(2):
                cache_f[b * 4 + e] = both[e * 64:e * 64 + 64].astype(BF16)
                cache_f[b * 4 + 2 + e] = values[e * 64:e * 64 + 64]

    cache_copy.wait()

    halves = [parts[h * 6:h * 6 + 5] for h in range(4)]
    zin = [parts[h * 6 + 5] for h in range(4)]
    pending = []

    def push(src, dst, ssem, rsem, where):
        cp = remote(src, dst, ssem, rsem, where)
        cp.start()
        pending.append(cp)

    def landed(ref, rsem):
        remote(ref, ref, y_ssem.at[0], rsem, sibling).wait_recv()

    own_y = []
    for h in (range(4) if "prefix" in ON else ()):
        yb = halves[h][0]
        split_cache(h)
        for d in (1, 3, 2):
            j = (y + d) % 4
            push(cache_f.at[pl.ds(j * 16 + h * 4, 4)], yb.at[y], y_ssem.at[h * 3 + d - 1], y_rsem.at[h * 3 + 3 - d], at_y(d))
        own_y.append(copy_here(cache_f.at[pl.ds(y * 16 + h * 4, 4)], yb.at[y]))

    oc = jnp.int32(-1)
    od = jnp.int32(-1)
    for p in range(4):
        o = owner_ref[p]
        inner = jnp.logical_and(o != 0, o != 31)
        fresh = oc < 0
        od = jnp.where(jnp.logical_and(inner, jnp.logical_not(fresh)), o, od)
        oc = jnp.where(jnp.logical_and(inner, fresh), o, oc)
    oc = jnp.clip(oc, 0, 31)
    od = jnp.clip(od, 0, 31)
    mine = jnp.where(c == 0, oc, od)
    theirs = jnp.where(c == 0, od, oc)

    def quarter(item, j, h):
        return f_out.at[item, pl.ds(j * 16 + h * 4, 4)]

    far = (zh - 3 * c) % 4

    def end_copy(h, d, src):
        return remote(src, quarter(c, y, h), a_ssem.at[h * 2 + d // 2], a_rsem.at[h], at_z(d))

    def stage_y(h):
        yb, sb, cb, zb, pb = halves[h]
        own_y[h].wait()
        for d in (1, 3, 2):
            landed(yb.at[(y + d) % 4], y_rsem.at[h * 3 + d - 1])
        sb[...] = yb[(theirs >> 1) & 3]
        push(sb, cb.at[c], b_ssem.at[h], b_rsem.at[h], sibling)

        @pl.when(far == 0)
        def _():
            end_copy(h, 1, yb.at[3 * c]).start()
            end_copy(h, 3, yb.at[3 * c]).start()
            pltpu.make_async_copy(yb.at[3 * c], quarter(c, y, h), e_sem.at[h]).start()

        cb[c] = yb[(mine >> 1) & 3]

    def unit(ref, d):
        return ref.at[(zh + 4 - d) % 4]

    def zsem(sem, h, n):
        return sem.at[h * 6 + n]

    def stage_core(h):
        yb, sb, cb, zb, pb = halves[h]
        landed(cb.at[other], b_rsem.at[h])
        zb[...] = cb[mine & 1]
        for d in (1, 3, 2):
            push(unit(zb, d), zin[h].at[d - 1], zsem(z_ssem, h, d - 1), zsem(z_rsem, h, d - 1), at_z(4 - d))

    zo = mine >> 3

    def stage_reduce(h):
        yb, sb, cb, zb, pb = halves[h]
        whole = zb[zh]
        for d in (1, 3, 2):
            landed(zin[h].at[d - 1], zsem(z_rsem, h, d - 1))
            whole = jnp.where(zo == (zh + d) % 4, zin[h][d - 1], whole)
        pb[zh] = whole
        for d in (1, 3, 2):
            push(unit(pb, 0), unit(pb, 0), zsem(z_ssem, h, 2 + d), zsem(z_rsem, h, 2 + d), at_z(d))

    def stage_relay(h):
        @pl.when(jnp.logical_or(far == 1, far == 3))
        def _():
            landed(quarter(c, y, h), a_rsem.at[h])

        @pl.when(far == (1 if h % 2 == 0 else 3))
        def _():
            end_copy(h, 1 if h % 2 == 0 else 3, quarter(c, y, h)).start()

    def relay(item, j, h, i, d):
        n = (i * 4 + d) * 4 + h
        push(quarter(item, j, h), quarter(item, j, h), r_ssem.at[n], r_rsem.at[n], sibling)

    def spread_own(h, i, src):
        item = c + 2 * i
        for d in (1, 3):
            push(src, quarter(item, y, h), t_ssem.at[(i * 3 + d - 1) * 4 + h], t_rsem.at[(i * 3 + 3 - d) * 4 + h], at_y(d))
        n = (i * 4) * 4 + h
        push(src, quarter(item, y, h), r_ssem.at[n], r_rsem.at[n], sibling)

    def stage_end(h):
        yb, sb, cb, zb, pb = halves[h]

        @pl.when(far == 2)
        def _():
            landed(quarter(c, y, h), a_rsem.at[h])

        @pl.when(far == 0)
        def _():
            pltpu.make_async_copy(yb.at[3 * c], quarter(c, y, h), e_sem.at[h]).wait()

        spread_own(h, 0, quarter(c, y, h))

    def stage_z(h):
        yb, sb, cb, zb, pb = halves[h]
        for d in (1, 3, 2):
            landed(unit(pb, d), zsem(z_rsem, h, 2 + d))
        copy_here(pb, quarter(c + 2, y, h))
        spread_own(h, 1, pb)

    def end_drain(h):
        @pl.when(far == 0)
        def _():
            end_copy(h, 1, quarter(c, y, h)).wait_send()
            end_copy(h, 3, quarter(c, y, h)).wait_send()

        @pl.when(far == (1 if h % 2 == 0 else 3))
        def _():
            end_copy(h, 1 if h % 2 == 0 else 3, quarter(c, y, h)).wait_send()

    def stage_spread(h):
        for i in range(2):
            item = c + 2 * i
            for d in (3, 1):
                j = (y + d) % 4
                landed(quarter(item, j, h), t_rsem.at[(i * 3 + d - 1) * 4 + h])
                if (i == 0 and d == 3) or (i == 1 and d == 1):
                    push(
                        quarter(item, j, h), quarter(item, j, h), t_ssem.at[(i * 3 + 1) * 4 + h], t_rsem.at[(i * 3 + 1) * 4 + h],
                        at_y(1 if i == 0 else 3),
                    )
                relay(item, j, h, i, d)

    def stage_far(h):
        for i in range(2):
            item = c + 2 * i
            j = (y + 2) % 4
            landed(quarter(item, j, h), t_rsem.at[(i * 3 + 1) * 4 + h])
            relay(item, j, h, i, 2)

    def rotary_tables():
        first, stop, _ = slot_tables(len_ref[...], order_ref[...], pref_ref[...])
        tok = (lax.broadcasted_iota(jnp.int32, (1, TOK), 1) + s * TOK).astype(F32)
        start = jnp.max(jnp.where(stop <= tok, jnp.broadcast_to(stop, (REQS, TOK)), 0.0), axis=0, keepdims=True)
        place = tok - start + float(PREFIX)
        angle = freq_ref[...] * place
        cos_buf[...] = jnp.cos(angle)
        sin_buf[...] = jnp.sin(angle)

    def turn_weights(i):
        @pl.loop(i * 9, i * 9 + 9)
        def _(f):
            rows = pl.ds(pl.multiple_of(f * 128, 128), 128)
            g = gain_ref[pl.ds(f, 1), :]
            for cb in range(4):
                w = w_buf[rows, cb * 128:(cb + 1) * 128].astype(F32).T
                wt[cb * 128:(cb + 1) * 128, rows] = (w * g).astype(BF16)

    def multiply(pair, g, begin):
        rows = pl.multiple_of(pair * 1152, 128)
        lanes = slice(g * 256, g * 256 + 256)
        for m in range(2):
            mm = slice(m * 256, m * 256 + 256)
            part = jnp.dot(wt[mm, pl.ds(rows, 1152)], h_buf[pl.ds(rows, 1152), lanes], preferred_element_type=F32)
            acc[mm, lanes] = part if begin else acc[mm, lanes] + part

        @pl.loop(0, 9)
        def _(b):
            v = h_buf[pl.ds(pl.multiple_of(rows + b * 128, 128), 128), lanes].astype(F32)
            v = v * v
            tot = v[0:8]
            for e in range(1, 16):
                tot = tot + v[e * 8:(e + 1) * 8]
            sq[:, lanes] = sq[:, lanes] + tot

    sq[...] = jnp.zeros_like(sq)
    for cp in weights:
        cp.wait()

    def turned(r0, g):
        lanes = slice(g * 256, g * 256 + 256)
        scale = lax.rsqrt(jnp.sum(sq[:, lanes], axis=0, keepdims=True) * (1.0 / WIDTH) + EPS)
        cos, sin = cos_buf[:, lanes], sin_buf[:, lanes]
        a = acc[r0:r0 + 64, lanes] * scale
        b = acc[r0 + 64:r0 + 128, lanes] * scale
        return a * cos - b * sin, b * cos + a * sin, scale

    def finish(g):
        a, b, scale = turned(256, g)
        kt = jnp.concatenate([a, b], axis=0)
        vt = (acc[384:512, g * 256:g * 256 + 256] * scale).astype(BF16)
        for e in range(2):
            kv_own[g * 2 + e, 0:128, :] = kt[:, e * 128:(e + 1) * 128].T.astype(BF16)
            kv_own[g * 2 + e, 128:256, :] = vt[:, e * 128:(e + 1) * 128]

    def queries(g):
        lanes = slice(g * 256, g * 256 + 256)
        for hd in range(2):
            a, b, _ = turned(hd * 128, g)
            q_out[hd * 128:hd * 128 + 64, lanes] = a.astype(BF16)
            q_out[hd * 128 + 64:hd * 128 + 128, lanes] = b.astype(BF16)

    def kv(slot, g):
        return kv_out.at[pl.ds(slot * 4 + g * 2, 2)]

    sib_slot = (4 * other, 4 - 2 * other, 2 - 2 * other)
    my_slot = (4 * c, 4 - 2 * c, 2 - 2 * c)

    def kv_way(n, g, src, dst, where):
        return remote(src, dst, k_ssem.at[n * 2 + g], k_rsem.at[n * 2 + g], where)

    def transit(g):
        return kv_via.at[pl.ds(g * 2, 2)]

    def kv_start(g):
        src = kv_own.at[pl.ds(g * 2, 2)]

        @pl.when(y >= 2)
        def _():
            kv_way(5, g, src, transit(g), at_z(1)).start()

        @pl.when(y <= 2)
        def _():
            kv_way(0, g, src, kv(3, g), at_y(1)).start()

        kv_way(2, g, src, kv(sib_slot[0], g), sibling).start()
        copy_here(src, kv_out.at[pl.ds(20 + g * 2, 2)])

    def kv_transit(g):
        @pl.when(y >= 2)
        def _():
            landed(transit(g), k_rsem.at[10 + g])
            kv_way(6, g, transit(g), kv(1, g), at_y(2)).start()

        @pl.when(y == 3)
        def _():
            kv_way(0, g, transit(g), kv(3, g), at_y(1)).start()

    passes = jnp.logical_or(y == 1, y == 2)

    def kv_first(g):
        landed(kv(3, g), k_rsem.at[g])

        @pl.when(passes)
        def _():
            kv_way(1, g, kv(3, g), kv(1, g), at_y(1)).start()

        kv_way(3, g, kv(3, g), kv(sib_slot[1], g), sibling).start()

    def kv_second(g):
        @pl.when(y >= 2)
        def _():
            landed(kv(1, g), k_rsem.at[2 + g])

        @pl.when(y <= 1)
        def _():
            landed(kv(1, g), k_rsem.at[12 + g])

        kv_way(4, g, kv(1, g), kv(sib_slot[2], g), sibling).start()

    def kv_drain(g):
        own = kv_own.at[pl.ds(g * 2, 2)]
        kv_way(0, g, own, kv(3, g), sibling).wait_send()
        for n in (2, 3, 4):
            kv_way(n, g, own, kv(3, g), sibling).wait_send()

        @pl.when(passes)
        def _():
            kv_way(1, g, own, kv(3, g), sibling).wait_send()

        @pl.when(y >= 2)
        def _():
            kv_way(5, g, own, kv(3, g), sibling).wait_send()
            kv_way(6, g, own, kv(3, g), sibling).wait_send()

    def both(step):
        def run(k):
            step(2 * k)
            step(2 * k + 1)

        return run

    steps = {
        "W": turn_weights, "g1": both(gather.first), "g2": both(gather.second), "g3": both(gather.third), "sy": stage_y, "sc": stage_core,
        "sr": stage_reduce, "er": stage_relay, "se": stage_end,
        "sz": stage_z, "sp": stage_spread, "sf": stage_far, "kt": kv_transit, "k1": kv_first, "k2": kv_second,
        "rot": lambda _: rotary_tables(), "kv": kv_start, "fin": finish, "q": queries, "gs": lambda _: gather.start(4, 8),
        "M": lambda i: multiply(
            (l * 2 + x // 2, l * 2 + 1 - x // 2, (1 - l) * 2 + x // 2, (1 - l) * 2 + 1 - x // 2)[i % 4], i // 4, i % 4 == 0
        ),
    }
    groups = {"W": "mm", "M": "mm", "rot": "mm", "fin": "mm", "q": "mm", "g1": "gather", "gs": "gather", "g2": "gather", "g3": "gather",
              "kv": "kv", "kt": "kv", "k1": "kv", "k2": "kv"}
    for name, arg in SCHED:
        if groups.get(name, "prefix") in ON:
            steps[name](arg)
    if "prefix" in ON:
        for i in range(2):
            item = other + 2 * i
            for d in range(4):
                for h in range(4):
                    landed(quarter(item, (y + d) % 4, h), r_rsem.at[(i * 4 + d) * 4 + h])
    if "kv" in ON:
        for n in range(3):
            for g in range(2):
                landed(kv(my_slot[n], g), k_rsem.at[4 + 2 * n + g])
    gather.drain()
    for cp in pending:
        cp.wait_send()
    if "kv" in ON:
        for g in range(2):
            kv_drain(g)
    if "prefix" in ON:
        for h in range(4):
            end_drain(h)
    for cp in local[5 + (4 if "prefix" in ON else 0):]:
        cp.wait()


def kernel_attend(
    owner_s, len_s, order_s, pref_s, len_ref, order_ref, pref_ref, q_ref, kv_ref, f_ref, out_ref, acc, meta, work, item_of
):
    base = lax.axis_index("seq") * TOK
    seen = jnp.int32(0)
    for p in range(4):
        o = owner_s[p]
        inner = jnp.logical_and(o != 0, o != 31)
        item_of[p] = jnp.where(o == 0, 0, jnp.where(o == 31, 1, 2 + jnp.minimum(seen, 1)))
        seen = seen + inner.astype(jnp.int32)

    def look(r, carry):
        at = carry[0]
        req = order_s[r]
        stop = at + len_s[req]
        bit = jnp.int32(1) << pref_s[req]
        out = [stop]
        for rb in range(4):
            lo = base + rb * 128
            hit = jnp.logical_and(at < lo + 128, stop > lo)
            out.append(jnp.where(hit, carry[1 + 2 * rb] | bit, carry[1 + 2 * rb]))
            out.append(jnp.where(jnp.logical_and(at <= lo, stop > lo), at, carry[2 + 2 * rb]))
        return tuple(out)

    zero = jnp.int32(0)
    found = lax.fori_loop(0, REQS, look, (zero,) * 9)
    count = jnp.int32(0)
    for rb in range(4):
        for p in range(4):
            work[count] = rb * 4 + p
            count = count + ((found[1 + 2 * rb] >> p) & 1)

    first, stop, prefix = slot_tables(len_ref[...], order_ref[...], pref_ref[...])
    for rb in range(4):
        tok = (lax.broadcasted_iota(jnp.int32, (1, 256), 1) % 128 + (base + rb * 128)).astype(F32)
        begin = jnp.max(jnp.where(stop <= tok, jnp.broadcast_to(stop, (REQS, 256)), 0.0), axis=0, keepdims=True)
        inside = jnp.logical_and(first <= tok, tok < stop)
        pref = jnp.sum(jnp.where(inside, jnp.broadcast_to(prefix, (REQS, 256)), 0.0), axis=0, keepdims=True)
        meta[rb, 0:1, :] = tok
        meta[rb, 1:2, :] = begin
        meta[rb, 2:3, :] = pref
    c1 = float(QSCALE ** -0.5 / SOFTCAP)
    c2 = float(SOFTCAP * math.log2(math.e))
    ones = jnp.ones((16, KEYS), BF16)

    def queries(rb):
        lanes = pl.ds(pl.multiple_of(rb * 128, 128), 128)
        return jnp.concatenate([q_ref[0:128, lanes], q_ref[128:256, lanes]], axis=1)

    def weigh(k2, qt):
        sc = jnp.dot(k2, qt, preferred_element_type=F32)
        return jnp.exp2(jnp.tanh(sc * c1) * c2)

    for rb in range(4):
        qt = queries(rb)
        tok = meta[rb, 0:1, :]
        begin = meta[rb, 1:2, :]
        acc[rb] = jnp.zeros((144, 256), F32)
        chunks = (base + (rb + 1) * 128 - found[2 + 2 * rb] + KEYS - 1) // KEYS

        @pl.loop(0, chunks)
        def _(n):
            u = 20 + rb + 1 - (n + 1) * (KEYS // 128)
            k2 = jnp.concatenate([kv_ref[u + e, 0:128, :] for e in range(KEYS // 128)], axis=0)
            v2 = jnp.concatenate([kv_ref[u + e, 128:256, :] for e in range(KEYS // 128)], axis=1)
            key = (lax.broadcasted_iota(jnp.int32, (KEYS, 1), 0) + (base - 2560 + u * 128)).astype(F32)
            ok = jnp.logical_and(key <= tok, key >= begin)
            w = jnp.where(ok, weigh(k2, qt), 0.0).astype(BF16)
            acc[rb] += jnp.dot(jnp.concatenate([v2, ones], axis=0), w, preferred_element_type=F32)

    @pl.loop(0, count)
    def _(i):
        code = work[i]
        rb, p = code >> 2, code & 3
        item = item_of[p]
        qt = queries(rb)
        ws = []
        vs = []
        for n in range(PREFIX // KEYS):
            u = n * (KEYS // 32)
            k2 = jnp.concatenate([f_ref[item, u + 4 * (e // 2) + e % 2] for e in range(KEYS // 64)], axis=0)
            vs += [
                jnp.concatenate([f_ref[item, u + 4 * e + 2], f_ref[item, u + 4 * e + 3]], axis=0) for e in range(KEYS // 128)
            ]
            ws.append(weigh(k2, qt).astype(BF16))
        v2 = jnp.concatenate([jnp.concatenate(vs, axis=1), jnp.ones((16, PREFIX), BF16)], axis=0)
        part = jnp.dot(v2, jnp.concatenate(ws, axis=0), preferred_element_type=F32)
        acc[rb] += jnp.where(meta[rb, 2:3, :] == p.astype(F32), part, 0.0)

    for rb in range(4):
        lanes = slice(rb * 128, rb * 128 + 128)
        att = acc[rb, 0:128, :] / acc[rb, 128:129, :]
        out_ref[0:128, lanes] = att[:, 0:128].astype(BF16)
        out_ref[128:256, lanes] = att[:, 128:256].astype(BF16)


def kernel_out(
    att_ref, wo_hbm, h_ref, gain_ref, out_ref, g_buf, wo_buf, acc, gcol, sums, g_ssem, g_rsem, q_ssem, q_rsem, local_sem
):
    s = lax.axis_index("seq")
    t = lax.axis_index("tp")
    l, x = t // 4, t % 4
    gather = Gather(OUT_PIECES, False, att_ref, g_buf, g_ssem, g_rsem, 256, x, l)

    def peer(d):
        return {"tp": (t + d) % 8}

    barrier = pltpu.get_barrier_semaphore()
    for d in range(1, 8):
        pl.semaphore_signal(barrier, inc=1, device_id=peer(d), device_id_type=MESH)
    wo_copy = pltpu.make_async_copy(wo_hbm, wo_buf, local_sem.at[0])
    own_copy = pltpu.make_async_copy(att_ref, g_buf.at[pl.ds(pl.multiple_of(t * 256, 256), 256)], local_sem.at[1])
    wo_copy.start()
    own_copy.start()
    pl.semaphore_wait(barrier, 7)
    gather.start(0, gather.n)

    g5 = gain_ref[t]
    for b in range(5):
        gcol[b * 128:(b + 1) * 128, :] = jnp.broadcast_to(g5[b:b + 1, :], (128, 128)).T
    wo_copy.wait()
    own_copy.wait()

    def multiply(dx, dl, begin):
        shard = ((l + dl) % 2) * 4 + (x + dx) % 4
        rows = pl.ds(pl.multiple_of(shard * 256, 256), 256)

        @pl.loop(0, 4)
        def _(m):
            mm = pl.ds(pl.multiple_of(m * 144, 16), 144)
            part = jnp.dot(wo_buf[mm, rows], g_buf[rows, :], preferred_element_type=F32)
            acc[mm, :] = part if begin else acc[mm, :] + part

    multiply(0, 0, True)
    for k in range(gather.n):
        gather.first(k)
    multiply(1, 0, False)
    multiply(3, 0, False)
    multiply(0, 1, False)
    for k in range(gather.n):
        gather.second(k)
    multiply(2, 0, False)
    multiply(1, 1, False)
    multiply(3, 1, False)
    for k in range(gather.n):
        gather.third(k)
    multiply(2, 1, False)

    tot = jnp.zeros((8, TOK), F32)
    for b in range(72):
        v = acc[b * 8:(b + 1) * 8, :]
        tot = tot + v * v
    sums[t] = jnp.sum(tot, axis=0, keepdims=True)
    copies = []
    for d in range(1, 8):
        cp = remote(sums.at[t], sums.at[t], q_ssem.at[d - 1], q_rsem.at[7 - d], peer(d))
        cp.start()
        copies.append(cp)
    for d in range(1, 8):
        here = sums.at[(t + d) % 8]
        remote(here, here, q_ssem.at[0], q_rsem.at[d - 1], peer(1)).wait_recv()
    tot = sums[0]
    for d in range(1, 8):
        tot = tot + sums[d]
    scale = lax.rsqrt(tot * (1.0 / WIDTH) + EPS)
    for b in range(9):
        rows = slice(b * 64, b * 64 + 64)
        g = gcol[rows, :]
        for n in range(4):
            cols = slice(n * 128, n * 128 + 128)
            post = acc[rows, cols] * scale[:, cols] * g
            out_ref[rows, cols] = (h_ref[rows, cols].astype(F32) + post).astype(BF16)
    gather.drain()
    for cp in copies:
        cp.wait_send()


def on_device(
    hidden_in, pre_gain, post_gain, w_query, key_weight, value_weight, w_out, cache, suffix_len, request_order,
    request_prefix, prefix_owner,
):
    hbm = pl.BlockSpec(memory_space=pltpu.MemorySpace.HBM)
    vmem = pl.BlockSpec(memory_space=pltpu.VMEM)
    smem = pl.BlockSpec(memory_space=pltpu.SMEM)
    dma = pltpu.SemaphoreType.DMA
    h_t = hidden_in.T
    len_row = suffix_len.reshape(1, REQS)
    order_row = request_order.reshape(1, REQS)
    pref_row = request_prefix.reshape(1, REQS)
    freq = jnp.asarray((10000.0 ** (-2.0 * np.arange(64) / HEAD)).astype(np.float32).reshape(64, 1))
    n = len(IN_PIECES)
    sends = 7 * n
    part = [
        pltpu.VMEM((4, 4, 64, 128), BF16), pltpu.VMEM((4, 64, 128), BF16), pltpu.VMEM((2, 4, 64, 128), BF16),
        pltpu.VMEM((4, 64, 128), BF16), pltpu.VMEM((4, 64, 128), BF16), pltpu.VMEM((3, 64, 128), BF16),
    ]
    q, kv, spread = pl.pallas_call(
        kernel_in,
        out_shape=(
            jax.ShapeDtypeStruct((256, TOK), BF16),
            jax.ShapeDtypeStruct((24, 256, 128), BF16),
            jax.ShapeDtypeStruct((4, 64, 64, 128), BF16),
        ),
        in_specs=[smem, vmem, vmem, vmem, vmem, vmem, hbm, hbm, hbm, hbm, hbm],
        out_specs=(vmem, vmem, vmem),
        scratch_shapes=[
            pltpu.VMEM((WIDTH, TOK), BF16),
            pltpu.VMEM((WIDTH, 512), BF16),
            pltpu.VMEM((512, WIDTH), BF16),
            pltpu.VMEM((512, TOK), F32),
            pltpu.VMEM((8, TOK), F32),
            pltpu.VMEM((64, TOK), F32),
            pltpu.VMEM((64, TOK), F32),
            pltpu.VMEM((4096, 128), BF16),
            pltpu.VMEM((64, 64, 128), BF16),
            *(part * 4),
            pltpu.VMEM((4, 256, 128), BF16), pltpu.VMEM((4, 256, 128), BF16),
            dma((sends,)), dma((8 * n,)), dma((12,)), dma((12,)), dma((4,)), dma((4,)), dma((24,)), dma((24,)),
            dma((24,)), dma((24,)), dma((8,)), dma((4,)), dma((4,)), dma((32,)), dma((32,)), dma((14,)), dma((14,)), dma((16,)),
        ],
        compiler_params=pltpu.CompilerParams(collective_id=0, has_side_effects=True, vmem_limit_bytes=34 << 20),
    )(
        *(
            pltpu.with_memory_space_constraint(a, pltpu.MemorySpace.HBM)
            for a in (
                prefix_owner, len_row, order_row, pref_row, pre_gain.reshape(36, 128), freq,
                h_t, w_query, key_weight, value_weight, cache.reshape(4096, 128),
            )
        )
    )
    att = pl.pallas_call(
        kernel_attend,
        out_shape=jax.ShapeDtypeStruct((256, TOK), BF16),
        in_specs=[smem] * 4 + [vmem] * 6,
        out_specs=vmem,
        scratch_shapes=[
            pltpu.VMEM((4, 144, 256), F32),
            pltpu.VMEM((4, 8, 256), F32),
            pltpu.SMEM((17,), jnp.int32),
            pltpu.SMEM((4,), jnp.int32),
        ],
        compiler_params=pltpu.CompilerParams(vmem_limit_bytes=16 << 20),
    )(prefix_owner, suffix_len, request_order, request_prefix, len_row, order_row, pref_row, q, kv, spread)
    gains = jnp.pad(post_gain.reshape(8, SHARD), ((0, 0), (0, 64))).reshape(8, 5, 128)
    out = pl.pallas_call(
        kernel_out,
        out_shape=jax.ShapeDtypeStruct((SHARD, TOK), BF16),
        in_specs=[vmem, hbm, vmem, vmem],
        out_specs=vmem,
        scratch_shapes=[
            pltpu.VMEM((2048, TOK), BF16),
            pltpu.VMEM((SHARD, 2048), BF16),
            pltpu.VMEM((SHARD, TOK), F32),
            pltpu.VMEM((640, 128), F32),
            pltpu.VMEM((8, 1, TOK), F32),
            dma((7 * len(OUT_PIECES),)), dma((8 * len(OUT_PIECES),)), dma((7,)), dma((7,)), dma((2,)),
        ],
        compiler_params=pltpu.CompilerParams(collective_id=1, has_side_effects=True, vmem_limit_bytes=16 << 20),
    )(att, w_out.T, h_t, gains)
    return out.T


def solution(mesh):
    placed = (
        P("seq", "tp"), P(), P(), P(None, "tp"), P(None, "tp"), P(None, "tp"), P(None, "tp"), P("seq", None, "tp"),
        P(), P(), P(), P(),
    )
    return jax.shard_map(on_device, mesh=mesh, in_specs=placed, out_specs=P("seq", "tp"), check_vma=False)
```
